256 devices in a mesh: row: 16 (over x, y), col: 16 (over z, core).
Axes of the slice: x: 4, y: 4, z: 8, core: 2. Of those that a mesh axis runs over, the one named last changes fastest.
Arguments:
- target: float32 [8, 16, 128, 8, 16, 128], P(None, 'row', None, None, 'col'), may hold values from -6 to 6
- panel_a: bfloat16 [2, 32, 128, 512], P(None, 'col'), may hold values from -1.1953125 to 1.1953125
- inv_factor: bfloat16 [2, 512, 512], replicated, as said below
- panel_rhs: bfloat16 [2, 512, 256], P(None, 'col'), may hold values from -6 to 6
- panel_rows: int32 [2, 32], replicated, may hold values from 0 to 127, as said below
- right_sides: float32 [8, 16, 128, 256], P(None, 'col'), may hold values from -12 to 12
Outputs:
- updated_target: float32 [8, 16, 128, 8, 16, 128], P(None, 'row', None, None, 'col')
- updated_sides: float32 [8, 16, 128, 256], P(None, 'col')
The draws below stay inside these ranges and needn't reach their ends.
Inputs may be any that keep to these rules, and one draw needn't show every extreme that they name: `panel_rows`: each row holds 32 distinct positions in increasing order, the first 0 and the last 127. `inv_factor`: lower triangular, diagonal between 0.5 and 2.
All inputs are finite; a program needn't handle non-finite values.
Results may differ from the reference program's by a relative error of at most 0.0035.
Values may be sent and summed in bfloat16 or wider, within the bound.
A program may use at most 128 MiB of HBM per device.

```python
import jax
import jax.numpy as jnp

TILE = 128
PW = 512
NRHS = 256
TPR = 8
U = 128
TPC = 8
R = 32
N_ROW = 16
N_COL = 16


def pick_positions(key):
    inner = jax.random.permutation(key, U - 2)[:R - 2].astype(jnp.int32) + 1
    first = jnp.zeros((1,), jnp.int32)
    last = jnp.full((1,), U - 1, jnp.int32)
    return jnp.sort(jnp.concatenate([first, inner, last]))


def draw_panel_rows(key, part):
    return jnp.stack([pick_positions(jax.random.fold_in(key, 11)), pick_positions(jax.random.fold_in(key, 12))])


def draw_inv_factor(key, part):
    key_low = jax.random.fold_in(key, 21)
    key_diag = jax.random.fold_in(key, 22)
    base = jax.random.normal(key_low, (2, PW, PW), jnp.float32) * PW ** (-0.5)
    lower = jnp.tril(base, -1)
    diagonal = jax.random.uniform(key_diag, (2, PW), jnp.float32, 0.5, 2.0)
    return (lower + diagonal[:, :, None] * jnp.eye(PW, dtype=jnp.float32)[None]).astype(jnp.bfloat16)


def levels(rng, extent, cuts, smallest, high):
    loudness = 1.0
    for dim, parts in cuts:
        draws = jax.random.uniform(jax.random.fold_in(jax.random.fold_in(rng, 6), dim), (parts,), jnp.float32, smallest / len(cuts), high / len(cuts))
        loudness = loudness * jnp.repeat(jnp.exp(draws), extent[dim] // parts).reshape((-1,) + (1,) * (len(extent) - 1 - dim))
    return loudness


def normal_values(stream_key, dims, width, reach, cuts=(), kind=jnp.bfloat16):
    result = jax.random.normal(stream_key, dims, jnp.float32) * width
    if len(cuts) > 0:
        result = levels(stream_key, dims, cuts, -0.22, 0.18) * result
    return jnp.clip(result, min=-reach, max=reach).astype(kind)


def setup_inputs(seed: int = 0) -> dict:
    arg_keys = jax.random.split(jax.random.key(seed), 7)
    target = normal_values(arg_keys[0], (TPR, N_ROW, TILE, TPC, N_COL, TILE), 1.0, 6.0, ((1, 16), (4, 16)), jnp.float32)
    panel_a = normal_values(arg_keys[1], (2, R, TILE, PW), 0.2, 1.1953125, ((1, 16),))
    inv_factor = draw_inv_factor(jax.random.fold_in(arg_keys[6], 71), 0)
    panel_rhs = normal_values(arg_keys[3], (2, PW, NRHS), 1.0, 6.0, ((1, 16),))
    panel_rows = draw_panel_rows(jax.random.fold_in(arg_keys[6], 71), 0)
    right_sides = normal_values(arg_keys[5], (TPC, N_COL, TILE, NRHS), 2.0, 12.0, ((1, 16),), jnp.float32)
    return dict(target=target, panel_a=panel_a, inv_factor=inv_factor, panel_rhs=panel_rhs, panel_rows=panel_rows, right_sides=right_sides)


def reference(target, panel_a, inv_factor, panel_rhs, panel_rows, right_sides):
    positions = TPR * N_ROW
    blocks = target.reshape(positions, TILE, positions, TILE)
    sides = right_sides.reshape(positions, TILE, NRHS)
    for which_panel in range(2):
        factor = inv_factor[which_panel].astype(jnp.float32)
        solved = jnp.einsum("axq,pq->axp", panel_a[which_panel].astype(jnp.float32), factor).astype(jnp.bfloat16)
        partial_value = jnp.dot(inv_factor[which_panel], panel_rhs[which_panel], preferred_element_type=jnp.float32).astype(jnp.bfloat16)
        flat = solved.astype(jnp.float32)
        gram = jnp.einsum("axp,byp->abxy", flat, flat)
        where = panel_rows[which_panel].astype(jnp.int32)
        blocks = blocks.at[where[:, None], :, where[None, :], :].add(-gram)
        sides = sides.at[where].add(-jnp.einsum("axp,pn->axn", flat, partial_value.astype(jnp.float32)))
    return blocks.reshape(target.shape), sides.reshape(right_sides.shape)
```

```python
import functools

import jax
import jax.numpy as jnp
from jax import lax
from jax.experimental import pallas as pl
from jax.experimental.pallas import tpu as pltpu
from jax.sharding import PartitionSpec as P

MESH = pl.DeviceIdType.MESH
NX, NY, NZ = 4, 4, 8
NROW, NCOL = 16, 16
SLOTS = 16
SLAB = 8
PW = 512
ZERO_BLOCK = 64


class Copies:
    def __init__(self):
        self.sent = []

    def start(self, src, dst, send_sem, recv_sem, device):
        copy = pltpu.make_async_remote_copy(
            src_ref=src,
            dst_ref=dst,
            send_sem=send_sem,
            recv_sem=recv_sem,
            device_id=device,
            device_id_type=MESH,
        )
        copy.start()
        self.sent.append(copy)

    def arrived(self, ref, send_sem, recv_sem, device):
        pltpu.make_async_remote_copy(
            src_ref=ref,
            dst_ref=ref,
            send_sem=send_sem,
            recv_sem=recv_sem,
            device_id=device,
            device_id_type=MESH,
        ).wait_recv()

    def finish(self):
        for copy in self.sent:
            copy.wait_send()


class ZRing:
    def __init__(self, copies, whole, half, place, send, recv, mate_send, mate_recv):
        self.copies, self.whole, self.half = copies, whole, half
        self.row, self.z, self.k = place
        self.send, self.recv = send, recv
        self.mate_send, self.mate_recv = mate_send, mate_recv

    def chip(self, distance):
        return lax.rem(self.z + distance + NZ, NZ)

    def device(self, distance):
        return (self.row, self.chip(distance) * 2 + self.k)

    def piece(self, core, way, hops):
        origin = self.chip(-hops if way == 0 else hops) * 2 + core
        return self.half(origin, way) if hops == NZ // 2 else self.whole(origin)

    def to_mate(self, way, hops):
        ref = self.piece(self.k, way, hops)
        at = way * 4 + hops
        self.copies.start(
            ref, ref, self.mate_send.at[at], self.mate_recv.at[at], (self.row, self.z * 2 + 1 - self.k)
        )

    def pass_on(self, way, hops):
        origin = self.chip(-hops if way == 0 else hops) * 2 + self.k
        ref = self.half(origin, way) if hops + 1 == NZ // 2 else self.whole(origin)
        self.copies.start(
            ref, ref, self.send.at[way, hops], self.recv.at[way, hops], self.device(1 if way == 0 else -1)
        )

    def begin(self):
        for way in range(2):
            self.pass_on(way, 0)
        self.to_mate(0, 0)

    def step(self, hops):
        for way in range(2):
            ref = self.piece(self.k, way, hops)
            self.copies.arrived(
                ref, self.send.at[way, hops - 1], self.recv.at[way, hops - 1], self.device(1 if way == 0 else -1)
            )
            if hops < NZ // 2:
                self.pass_on(way, hops)
            self.to_mate(way, hops)

    def end(self):
        mate = (self.row, self.z * 2 + 1 - self.k)
        for way in range(2):
            for hops in range(way, NZ // 2 + 1):
                ref = self.piece(1 - self.k, way, hops)
                at = way * 4 + hops
                self.copies.arrived(ref, self.mate_send.at[at], self.mate_recv.at[at], mate)


class PlaneGather:
    def __init__(self, copies, cols, half, place, send1, recv1, send2, recv2):
        self.copies, self.cols, self.half = copies, cols, half
        self.x, self.y, self.col = place
        self.send1, self.recv1, self.send2, self.recv2 = send1, recv1, send2, recv2

    def row(self, along, across):
        dx, dy = (along, across) if self.half == 0 else (across, along)
        return lax.rem(self.x + dx + NX, NX) * NY + lax.rem(self.y + dy + NY, NY)

    def device(self, along, across):
        return (self.row(along, across), self.col)

    def ref(self, along, across, part):
        start = self.half * 8 + (0 if part is None else part * 4)
        return self.cols.at[self.row(along, across), pl.ds(start, 8 if part is None else 4)]

    def shift(self, item):
        return (0, -1, 1, 2, 2)[item]

    def part(self, item):
        return (None, None, None, 0, 1)[item]

    def across_send(self, item):
        for way in range(2):
            ref = self.ref(self.shift(item), 0, self.part(item))
            self.copies.start(
                ref,
                ref,
                self.send2.at[item, way, 0],
                self.recv2.at[item, way, 0],
                self.device(0, 1 if way == 0 else -1),
            )

    def begin(self):
        for way in range(2):
            ref = self.ref(0, 0, None)
            self.copies.start(
                ref, ref, self.send1.at[way, 0], self.recv1.at[way, 0], self.device(1 if way == 0 else -1, 0)
            )
        self.across_send(0)

    def near(self, way):
        towards = 1 if way == 0 else -1
        self.copies.arrived(
            self.ref(-towards, 0, None), self.send1.at[way, 0], self.recv1.at[way, 0], self.device(towards, 0)
        )
        ref = self.ref(-towards, 0, way)
        self.copies.start(
            ref, ref, self.send1.at[way, 1], self.recv1.at[way, 1], self.device(towards, 0)
        )
        self.across_send(1 + way)

    def far(self, way):
        towards = 1 if way == 0 else -1
        self.copies.arrived(
            self.ref(2, 0, way), self.send1.at[way, 1], self.recv1.at[way, 1], self.device(towards, 0)
        )
        self.across_send(3 + way)

    def across_near(self, item):
        for way in range(2):
            towards = 1 if way == 0 else -1
            self.copies.arrived(
                self.ref(self.shift(item), -towards, self.part(item)),
                self.send2.at[item, way, 0],
                self.recv2.at[item, way, 0],
                self.device(0, towards),
            )
            if item < 3 or item - 3 == way:
                ref = self.ref(self.shift(item), -towards, way)
                self.copies.start(
                    ref, ref, self.send2.at[item, way, 1], self.recv2.at[item, way, 1], self.device(0, towards)
                )

    def across_far(self, item):
        for way in range(2):
            if item < 3 or item - 3 == way:
                self.copies.arrived(
                    self.ref(self.shift(item), 2, way),
                    self.send2.at[item, way, 1],
                    self.recv2.at[item, way, 1],
                    self.device(0, 1 if way == 0 else -1),
                )


def gather_kernel(
    table, panel, inv_factor, rhs,
    rows, cols, sides,
    slab, solved, picked, local_sem,
    ring1, ring1_in, mate1, mate1_in,
    ring2, ring2_in, mate2, mate2_in,
    ring3, ring3_in, mate3, mate3_in,
    swap, swap_in, plane1, plane1_in, plane2, plane2_in,
):
    row = lax.axis_index("row")
    col = lax.axis_index("col")
    x, y = row // NY, lax.rem(row, NY)
    z, k = col // 2, lax.rem(col, 2)
    place = (row, z, k)

    loads = []
    for q in range(2):
        for b in range(2):
            load = pltpu.make_async_copy(
                panel.at[q, b, pl.ds(pl.multiple_of(row * SLAB, SLAB), SLAB)], slab.at[q, b], local_sem.at[q, b]
            )
            load.start()
            loads.append(load)

    barrier = pltpu.get_barrier_semaphore()
    partners = [(row, lax.rem(z + 1, NZ) * 2 + k), (row, lax.rem(z + NZ - 1, NZ) * 2 + k), (row, z * 2 + 1 - k)]
    partners += [(lax.rem(row + d, NROW), col) for d in range(1, NROW)]
    for partner in partners:
        pl.semaphore_signal(barrier, inc=1, device_id=partner, device_id_type=MESH)

    solved[ZERO_BLOCK] = jnp.zeros((SLAB, PW), jnp.bfloat16)
    sides[col] = rhs[...]
    for load in loads:
        load.wait()
    for q in range(2):
        block = slab[q].astype(jnp.float32).reshape(2 * SLAB, PW).astype(jnp.bfloat16)
        value = lax.dot_general(
            block, inv_factor[q], (((1,), (1,)), ((), ())), preferred_element_type=jnp.float32
        )
        for b in range(2):
            solved[col * 4 + q * 2 + b] = value[b * SLAB:(b + 1) * SLAB].astype(jnp.bfloat16)

    pl.semaphore_wait(barrier, len(partners))

    copies = Copies()
    slabs = ZRing(
        copies,
        lambda origin: solved.at[pl.ds(origin * 4, 4)],
        lambda origin, way: solved.at[pl.ds(origin * 4 + way * 2, 2)],
        place, ring1, ring1_in, mate1, mate1_in,
    )
    side_ring = ZRing(
        copies,
        lambda origin: sides.at[origin],
        lambda origin, way: sides.at[origin, way],
        place, ring2, ring2_in, mate2, mate2_in,
    )
    row_rings = [
        ZRing(
            copies,
            lambda origin, n=n: rows.at[origin, pl.ds(n * 8, 8)],
            lambda origin, way, n=n: rows.at[origin, pl.ds(n * 8 + way * 4, 4)],
            place, ring3.at[n], ring3_in.at[n], mate3.at[n], mate3_in.at[n],
        )
        for n in range(2)
    ]
    planes = [
        PlaneGather(
            copies, cols, half, (x, y, col), plane1.at[half], plane1_in.at[half], plane2.at[half], plane2_in.at[half]
        )
        for half in range(2)
    ]

    slabs.begin()
    side_ring.begin()
    slabs.step(1)
    slabs.step(2)
    side_ring.step(1)
    slabs.step(3)
    slabs.step(4)
    slabs.end()

    for d in range(1, NROW):
        there = lax.rem(row + d, NROW)
        picked[d] = solved[table[SLOTS + there]]
        copies.start(picked.at[d], rows.at[col, row], swap.at[d], swap_in.at[d], (there, col))
    rows[col, row] = solved[table[SLOTS + row]]
    for slot in range(SLOTS):
        cols[row, slot] = solved[table[slot]]
    for plane in planes:
        plane.begin()
    side_ring.step(2)
    for d in range(1, NROW):
        origin = lax.rem(row + NROW - d, NROW)
        copies.arrived(rows.at[col, origin], swap.at[d], swap_in.at[d], (origin, col))
    for ring in row_rings:
        ring.begin()
    side_ring.step(3)
    for plane in planes:
        plane.near(0)
        plane.near(1)
    for plane in planes:
        plane.across_near(0)
    for ring in row_rings:
        ring.step(1)
    for plane in planes:
        plane.far(0)
        plane.far(1)
    for plane in planes:
        plane.across_near(1)
    for ring in row_rings:
        ring.step(2)
    for plane in planes:
        plane.across_near(2)
    for ring in row_rings:
        ring.step(3)
    for plane in planes:
        plane.across_near(3)
        plane.across_near(4)
    side_ring.step(4)
    for ring in row_rings:
        ring.step(4)
    for item in range(5):
        for plane in planes:
            plane.across_far(item)
    side_ring.end()
    for ring in row_rings:
        ring.end()
    copies.finish()


def gather(table, panel, inv_factor, rhs):
    dma = pltpu.SemaphoreType.DMA
    vmem = pl.BlockSpec(memory_space=pltpu.VMEM)
    return pl.pallas_call(
        gather_kernel,
        out_shape=(
            jax.ShapeDtypeStruct((SLOTS, NROW, SLAB, PW), jnp.bfloat16),
            jax.ShapeDtypeStruct((NROW, SLOTS, SLAB, PW), jnp.bfloat16),
            jax.ShapeDtypeStruct((NCOL,) + rhs.shape, jnp.bfloat16),
        ),
        in_specs=[
            pl.BlockSpec(memory_space=pltpu.SMEM),
            pl.BlockSpec(memory_space=pl.ANY),
            vmem,
            vmem,
        ],
        out_specs=(vmem, vmem, vmem),
        scratch_shapes=[
            pltpu.VMEM((2, 2, SLAB, PW), jnp.bfloat16),
            pltpu.VMEM((ZERO_BLOCK + 1, SLAB, PW), jnp.bfloat16),
            pltpu.VMEM((NROW, SLAB, PW), jnp.bfloat16),
            dma((2, 2)),
            dma((2, 4)), dma((2, 4)), dma((9,)), dma((9,)),
            dma((2, 4)), dma((2, 4)), dma((9,)), dma((9,)),
            dma((2, 2, 4)), dma((2, 2, 4)), dma((2, 9)), dma((2, 9)),
            dma((16,)), dma((16,)),
            dma((2, 2, 2)), dma((2, 2, 2)), dma((2, 5, 2, 2)), dma((2, 5, 2, 2)),
        ],
        compiler_params=pltpu.CompilerParams(
            collective_id=0, has_side_effects=True, vmem_limit_bytes=16 << 20
        ),
        name="gather_blocks",
    )(table, panel, inv_factor, rhs)


def update_kernel(rows, cols, inv_factor, rhs, target, right_sides, out_target, out_sides, partial, factors):
    step = pl.program_id(0)

    @pl.when(step == 0)
    def _():
        for q in range(2):
            value = jnp.dot(
                inv_factor[q], rhs[:, q].reshape(PW, rhs.shape[-1]), preferred_element_type=jnp.float32
            )
            partial[q] = value.astype(jnp.bfloat16)
            for s in range(8):
                factors[q, pl.ds(s * 128, 128), :] = cols[:, q * 8 + s].reshape(128, PW)

    tiles = target.shape[0]
    left = [rows[q].reshape(tiles * 128, PW) for q in range(2)]
    for pair in range(4):
        product = 0.0
        for q in range(2):
            product += lax.dot_general(
                left[q],
                factors[q, pl.ds(pair * 256, 256), :],
                (((1,), (1,)), ((), ())),
                preferred_element_type=jnp.float32,
            )
        for n in range(2):
            s = pair * 2 + n
            for t in range(tiles):
                at = (t, pl.ds(s, 128, 8), slice(None))
                out_target[at] = target[at] - product[t * 128:(t + 1) * 128, n * 128:(n + 1) * 128]
    for n in range(right_sides.shape[0]):
        start = pl.multiple_of((step * right_sides.shape[0] + n) * 128, 128)
        product = 0.0
        for q in range(2):
            product += jnp.dot(
                factors[q, pl.ds(start, 128), :], partial[q], preferred_element_type=jnp.float32
            )
        out_sides[n] = right_sides[n] - product


def update(rows, cols, inv_factor, rhs, target, right_sides):
    steps = 4
    each = 8 // steps
    whole = lambda shape: pl.BlockSpec(shape, lambda i: (0,) * len(shape))
    return pl.pallas_call(
        update_kernel,
        grid=(steps,),
        out_shape=(
            jax.ShapeDtypeStruct(target.shape, jnp.float32),
            jax.ShapeDtypeStruct(right_sides.shape, jnp.float32),
        ),
        in_specs=[
            pl.BlockSpec((2, each, 128, PW), lambda i: (0, i, 0, 0)),
            whole(cols.shape),
            whole(inv_factor.shape),
            whole(rhs.shape),
            pl.BlockSpec((each,) + target.shape[1:], lambda i: (i, 0, 0)),
            pl.BlockSpec((each,) + right_sides.shape[1:], lambda i: (i, 0, 0)),
        ],
        out_specs=(
            pl.BlockSpec((each,) + target.shape[1:], lambda i: (i, 0, 0)),
            pl.BlockSpec((each,) + right_sides.shape[1:], lambda i: (i, 0, 0)),
        ),
        scratch_shapes=[
            pltpu.VMEM((2, PW, rhs.shape[-1]), jnp.bfloat16),
            pltpu.VMEM((2, 1024, PW), jnp.bfloat16),
        ],
        compiler_params=pltpu.CompilerParams(
            dimension_semantics=("arbitrary",), vmem_limit_bytes=24 << 20
        ),
        name="update_blocks",
    )(rows, cols, inv_factor, rhs, target, right_sides)


def block_table(panel_rows):
    col = lax.axis_index("col")
    entry = jnp.arange(2 * SLOTS, dtype=jnp.int32)
    first = entry < SLOTS
    slot = jnp.where(first, entry, col)
    position = (slot % 8) * 16 + jnp.where(first, col, entry - SLOTS)
    panel = slot // 8
    positions = jnp.where((panel == 0)[:, None], panel_rows[0][None], panel_rows[1][None])
    block = jnp.arange(panel_rows.shape[1], dtype=jnp.int32)
    place = (block // 2) * 4 + block % 2
    found = positions == position[:, None]
    return ZERO_BLOCK + jnp.sum(
        jnp.where(found, place[None] + panel[:, None] * 2 - ZERO_BLOCK, 0), axis=1, dtype=jnp.int32
    )


def shards(target, panel_a, inv_factor, panel_rhs, panel_rows, right_sides):
    table = block_table(panel_rows)
    rows, cols, rhs = gather(table, panel_a, inv_factor, panel_rhs)
    new_target, new_sides = update(
        rows.reshape(2, 8, 128, PW),
        cols,
        inv_factor,
        rhs,
        target.reshape(8, 1024, 128),
        right_sides.reshape(8, 128, 256),
    )
    return new_target.reshape(target.shape), new_sides.reshape(right_sides.shape)


def solution(mesh):
    placed = (
        P(None, "row", None, None, "col", None),
        P(None, "col", None, None),
        P(),
        P(None, "col", None),
        P(),
        P(None, "col", None, None),
    )
    return jax.shard_map(
        shards,
        mesh=mesh,
        in_specs=placed,
        out_specs=(P(None, "row", None, None, "col", None), P(None, "col", None, None)),
        check_vma=False,
    )
```

```python
import functools

import jax
import jax.numpy as jnp
from jax import lax
from jax.experimental import pallas as pl
from jax.experimental.pallas import tpu as pltpu
from jax.sharding import PartitionSpec as P

MESH = pl.DeviceIdType.MESH
NX, NY, NZ = 4, 4, 8
NROW, NCOL = 16, 16
SLAB = 8
PW = 512
NRHS = 256
TILE = 128
ZERO_BLOCK = 64
NEAREST = (1, 7, 2, 6, 3, 5, 4)


def remote(src, dst, send_sem, recv_sem, device):
    return pltpu.make_async_remote_copy(
        src_ref=src, dst_ref=dst, send_sem=send_sem, recv_sem=recv_sem, device_id=device, device_id_type=MESH
    )


class Copies:
    def __init__(self):
        self.sent = []

    def start(self, ref, send_sem, recv_sem, device):
        copy = remote(ref, ref, send_sem, recv_sem, device)
        copy.start()
        self.sent.append(copy)

    def arrived(self, ref, send_sem, recv_sem, device):
        remote(ref, ref, send_sem, recv_sem, device).wait_recv()

    def finish(self):
        for copy in self.sent:
            copy.wait_send()


class ZGather:
    def __init__(self, copies, piece, place, send, recv, mate_send, mate_recv):
        self.copies, self.piece = copies, piece
        self.row, self.z, self.k = place
        self.send, self.recv = send, recv
        self.mate_send, self.mate_recv = mate_send, mate_recv
        self.mate = (self.row, self.z * 2 + 1 - self.k)

    def chip(self, distance):
        return lax.rem(self.z + distance + NZ, NZ)

    def begin(self):
        own = self.piece(self.z * 2 + self.k)
        for d in NEAREST:
            self.copies.start(own, self.send.at[d], self.recv.at[d], (self.row, self.chip(d) * 2 + self.k))
        self.copies.start(own, self.mate_send.at[0], self.mate_recv.at[0], self.mate)

    def collect(self):
        for d in NEAREST:
            ref = self.piece(self.chip(-d) * 2 + self.k)
            self.copies.arrived(ref, self.send.at[d], self.recv.at[d], (self.row, self.chip(d) * 2 + self.k))
            self.copies.start(ref, self.mate_send.at[d], self.mate_recv.at[d], self.mate)

    def end(self):
        for d in (0,) + NEAREST:
            ref = self.piece(self.chip(-d) * 2 + 1 - self.k)
            self.copies.arrived(ref, self.mate_send.at[d], self.mate_recv.at[d], self.mate)


class PlaneGather:
    def __init__(self, copies, cols, half, place, send1, recv1, send2, recv2):
        self.copies, self.cols, self.half = copies, cols, half
        self.x, self.y, self.col = place
        self.send1, self.recv1, self.send2, self.recv2 = send1, recv1, send2, recv2
        count = cols.shape[1] // 2
        self.count, self.lead = count, (count + 1) // 2

    def row(self, along, across):
        dx, dy = (along, across) if self.half == 0 else (across, along)
        return lax.rem(self.x + dx + NX, NX) * NY + lax.rem(self.y + dy + NY, NY)

    def device(self, along, across):
        return (self.row(along, across), self.col)

    def ref(self, along, across, part):
        start = self.half * self.count + (self.lead if part == 1 else 0)
        size = {None: self.count, 0: self.lead, 1: self.count - self.lead}[part]
        return self.cols.at[self.row(along, across), pl.ds(start, size)]

    def shift(self, item):
        return (0, -1, 1, 2, 2)[item]

    def part(self, item):
        return (None, None, None, 0, 1)[item]

    def across_send(self, item):
        for way in range(2):
            self.copies.start(
                self.ref(self.shift(item), 0, self.part(item)),
                self.send2.at[item, way, 0],
                self.recv2.at[item, way, 0],
                self.device(0, 1 if way == 0 else -1),
            )

    def begin(self):
        for way in range(2):
            self.copies.start(
                self.ref(0, 0, None), self.send1.at[way, 0], self.recv1.at[way, 0], self.device(1 if way == 0 else -1, 0)
            )
        self.across_send(0)

    def near(self, way):
        towards = 1 if way == 0 else -1
        self.copies.arrived(
            self.ref(-towards, 0, None), self.send1.at[way, 0], self.recv1.at[way, 0], self.device(towards, 0)
        )
        self.copies.start(
            self.ref(-towards, 0, way), self.send1.at[way, 1], self.recv1.at[way, 1], self.device(towards, 0)
        )
        self.across_send(1 + way)

    def far(self, way):
        towards = 1 if way == 0 else -1
        self.copies.arrived(
            self.ref(2, 0, way), self.send1.at[way, 1], self.recv1.at[way, 1], self.device(towards, 0)
        )
        self.across_send(3 + way)

    def across_near(self, item):
        for way in range(2):
            towards = 1 if way == 0 else -1
            self.copies.arrived(
                self.ref(self.shift(item), -towards, self.part(item)),
                self.send2.at[item, way, 0],
                self.recv2.at[item, way, 0],
                self.device(0, towards),
            )
            if item < 3 or item - 3 == way:
                self.copies.start(
                    self.ref(self.shift(item), -towards, way),
                    self.send2.at[item, way, 1],
                    self.recv2.at[item, way, 1],
                    self.device(0, towards),
                )

    def across_far(self, item):
        for way in range(2):
            if item < 3 or item - 3 == way:
                self.copies.arrived(
                    self.ref(self.shift(item), 2, way),
                    self.send2.at[item, way, 1],
                    self.recv2.at[item, way, 1],
                    self.device(0, 1 if way == 0 else -1),
                )


def class_tables(panel_rows):
    count = panel_rows.shape[1]
    shape = (count, count)
    down = lax.broadcasted_iota(jnp.int32, shape, 0)
    across = lax.broadcasted_iota(jnp.int32, shape, 1)
    lane = lax.broadcasted_iota(jnp.int32, (count, 256), 1)
    block = lax.broadcasted_iota(jnp.int32, (count, 256), 0)
    wide = [jnp.broadcast_to(panel_rows[q:q + 1], shape) for q in range(2)]
    tall = [jnp.sum(jnp.where(down == across, w, 0), axis=1, keepdims=True) for w in wide]
    place, info, total = ZERO_BLOCK, 0, 0
    for q in range(2):
        same = (tall[q] & 15) == (wide[q] & 15)
        rank = jnp.sum(jnp.where(same & (across < down), 1, 0), axis=1, keepdims=True)
        if q == 1:
            rank += jnp.sum(jnp.where((tall[1] & 15) == (wide[0] & 15), 1, 0), axis=1, keepdims=True)
        hit = jnp.broadcast_to((tall[q] & 15) * 16 + rank, lane.shape) == lane
        where_from = (block >> 1) * 4 + (block & 1) + q * 2
        place += jnp.sum(jnp.where(hit, where_from - ZERO_BLOCK, 0), axis=0, keepdims=True)
        spot = jnp.broadcast_to((tall[q] >> 4) + q * 8, lane.shape)
        info += jnp.sum(jnp.where(hit, spot, 0), axis=0, keepdims=True)
        member = jnp.broadcast_to(tall[q] & 15, lane.shape) == (lane >> 4)
        total += jnp.sum(jnp.where(member, 1, 0), axis=0, keepdims=True)
    return place, info, total


def gather_kernel(
    slots,
    positions_hbm, panel, inv_hbm, rhs, target, right_sides,
    rows, cols, partial, meta, target_copy, sides_copy,
    positions, slab, inv_factor, solved, picked, sides, table, local_sem,
    z1, z1_in, mate1, mate1_in, z2, z2_in, mate2, mate2_in,
    swap, swap_in, hand, hand_in, plane1, plane1_in, plane2, plane2_in,
):
    row = lax.axis_index("row")
    col = lax.axis_index("col")
    x, y = row // NY, lax.rem(row, NY)
    z, k = col // 2, lax.rem(col, 2)
    place = (row, z, k)
    mate = (row, z * 2 + 1 - k)

    def load(src, dst, n):
        copy = pltpu.make_async_copy(src, dst, local_sem.at[n])
        copy.start()
        return copy

    own_rows = pl.ds(pl.multiple_of(row * SLAB, SLAB), SLAB)
    first = [load(panel.at[q, b, own_rows], slab.at[q, b], 2 * q + b) for q in range(2) for b in range(2)]
    first += [load(inv_hbm, inv_factor, 4)]
    second = [load(rhs, sides.at[col], 5), load(positions_hbm, positions, 9)]

    barrier = pltpu.get_barrier_semaphore()
    partners = [(row, lax.rem(z + d, NZ) * 2 + k) for d in NEAREST] + [mate]
    partners += [(lax.rem(row + d, NROW), col) for d in range(1, NROW)]
    for partner in partners:
        pl.semaphore_signal(barrier, inc=1, device_id=partner, device_id_type=MESH)

    solved[ZERO_BLOCK] = jnp.zeros((SLAB, PW), jnp.bfloat16)
    for copy in first:
        copy.wait()
    for q in range(2):
        block = slab[q].astype(jnp.float32).reshape(2 * SLAB, PW).astype(jnp.bfloat16)
        value = lax.dot_general(
            block, inv_factor[q], (((1,), (1,)), ((), ())), preferred_element_type=jnp.float32
        )
        for b in range(2):
            solved[col * 4 + q * 2 + b] = value[b * SLAB:(b + 1) * SLAB].astype(jnp.bfloat16)
    for copy in second:
        copy.wait()

    pl.semaphore_wait(barrier, len(partners))

    copies = Copies()
    slabs = ZGather(
        copies, lambda origin: solved.at[pl.ds(origin * 4, 4)], place, z1, z1_in, mate1, mate1_in
    )
    side_parts = ZGather(copies, lambda origin: sides.at[origin], place, z2, z2_in, mate2, mate2_in)
    planes = [
        PlaneGather(
            copies, cols, half, (x, y, col), plane1.at[half], plane1_in.at[half], plane2.at[half], plane2_in.at[half]
        )
        for half in range(2)
    ]

    slabs.begin()
    side_parts.begin()
    late = [load(target, target_copy, 6), load(right_sides, sides_copy, 7)]
    for n, values in enumerate(class_tables(positions[...])):
        meta[n:n + 1, :] = values
    to_scalars = load(meta, table, 8)
    to_scalars.wait()
    slabs.collect()
    slabs.end()

    for slot in range(slots):
        cols[row, slot] = solved[table[0, col * 16 + slot]]
    for plane in planes:
        plane.begin()

    share = slots // 2
    own_share = pl.ds(k * share, share)

    def send_picked(d, carry):
        there = lax.rem(row + d, NROW)
        for j in range(share):
            picked[d, j] = solved[table[0, there * 16 + k * share + j]]
        remote(picked.at[d], rows.at[row, own_share], swap.at[d], swap_in.at[d], (there, col)).start()
        return carry

    lax.fori_loop(1, NROW, send_picked, 0)
    for j in range(share):
        rows[row, k * share + j] = solved[table[0, row * 16 + k * share + j]]

    def hand_over(origin, d):
        ref = rows.at[origin, own_share]
        remote(ref, ref, hand.at[d], hand_in.at[d], mate).start()

    def receive_picked(d, carry):
        origin = lax.rem(row + NROW - d, NROW)
        ref = rows.at[origin, own_share]
        remote(picked.at[d], ref, swap.at[d], swap_in.at[d], (lax.rem(row + d, NROW), col)).wait()
        hand_over(origin, d)
        return carry

    hand_over(row, 0)
    for plane in planes:
        plane.near(0)
        plane.near(1)
    side_parts.collect()
    for plane in planes:
        plane.across_near(0)
    for plane in planes:
        plane.far(0)
        plane.far(1)
    for plane in planes:
        plane.across_near(1)
        plane.across_near(2)
    lax.fori_loop(1, NROW, receive_picked, 0)
    for plane in planes:
        plane.across_near(3)
        plane.across_near(4)
    side_parts.end()
    for q in range(2):
        value = jnp.dot(
            inv_factor[q], sides[:, q].reshape(PW, NRHS), preferred_element_type=jnp.float32
        )
        partial[q] = value.astype(jnp.bfloat16)

    def take_over(d, carry):
        origin = lax.rem(row + NROW - d, NROW)
        ref = rows.at[origin, pl.ds((1 - k) * share, share)]
        remote(ref, ref, hand.at[d], hand_in.at[d], mate).wait()
        return carry

    lax.fori_loop(0, NROW, take_over, 0)
    for item in range(5):
        for plane in planes:
            plane.across_far(item)
    for copy in late:
        copy.wait()
    copies.finish()


def gather(slots, panel_rows, panel, inv_factor, rhs, target, right_sides):
    dma = pltpu.SemaphoreType.DMA
    vmem = pl.BlockSpec(memory_space=pltpu.VMEM)
    hbm = pl.BlockSpec(memory_space=pltpu.MemorySpace.HBM)
    return pl.pallas_call(
        functools.partial(gather_kernel, slots),
        out_shape=(
            jax.ShapeDtypeStruct((NROW, slots, SLAB, PW), jnp.bfloat16),
            jax.ShapeDtypeStruct((NROW, slots, SLAB, PW), jnp.bfloat16),
            jax.ShapeDtypeStruct((2, PW, NRHS), jnp.bfloat16),
            jax.ShapeDtypeStruct((8, 256), jnp.int32),
            jax.ShapeDtypeStruct(target.shape, jnp.float32),
            jax.ShapeDtypeStruct(right_sides.shape, jnp.float32),
        ),
        in_specs=[hbm] * 6,
        out_specs=(vmem,) * 6,
        scratch_shapes=[
            pltpu.VMEM(panel_rows.shape, jnp.int32),
            pltpu.VMEM((2, 2, SLAB, PW), jnp.bfloat16),
            pltpu.VMEM((2, PW, PW), jnp.bfloat16),
            pltpu.VMEM((ZERO_BLOCK + 1, SLAB, PW), jnp.bfloat16),
            pltpu.VMEM((NROW, slots // 2, SLAB, PW), jnp.bfloat16),
            pltpu.VMEM((NCOL,) + rhs.shape, jnp.bfloat16),
            pltpu.SMEM((8, 256), jnp.int32),
            dma((10,)),
            dma((8,)), dma((8,)), dma((8,)), dma((8,)),
            dma((8,)), dma((8,)), dma((8,)), dma((8,)),
            dma((16,)), dma((16,)), dma((16,)), dma((16,)),
            dma((2, 2, 2)), dma((2, 2, 2)), dma((2, 5, 2, 2)), dma((2, 5, 2, 2)),
        ],
        compiler_params=pltpu.CompilerParams(
            collective_id=0, has_side_effects=True, vmem_limit_bytes=24 << 20
        ),
        name="gather_blocks",
    )(
        *[
            pltpu.with_memory_space_constraint(array, pltpu.MemorySpace.HBM)
            for array in (panel_rows, panel, inv_factor, rhs, target, right_sides)
        ]
    )


def update_kernel(
    slots,
    meta, rows, cols, partial, target, right_sides,
    out_target, out_sides,
    tiles, sides, left, right, tile_sem, side_sem,
):
    row = lax.axis_index("row") * 16
    col = lax.axis_index("col") * 16
    rows_here = meta[2, row]
    cols_here = meta[2, col]
    count = target.shape[0]

    def touched(base, total):
        bits = jnp.int32(0)
        for i in range(slots):
            bits |= jnp.where(i < total, jnp.int32(1) << (meta[1, base + i] & 7), 0)
        return bits

    row_bits = touched(row, rows_here)

    def send_tile(source, t):
        return pltpu.make_async_copy(source.at[t], out_target.at[t], tile_sem.at[t])

    for t in range(count):
        @pl.when(((row_bits >> t) & 1) == 0)
        def _():
            send_tile(target, t).start()

        @pl.when(((row_bits >> t) & 1) == 1)
        def _():
            tiles[t] = target[t]

    for i in range(slots):
        @pl.when(i < ((rows_here + 1) // 2) * 2)
        def _():
            left[i * TILE:(i + 1) * TILE, :] = rows[:, i].reshape(TILE, PW)

        @pl.when(i < ((cols_here + 1) // 2) * 2)
        def _():
            right[i * TILE:(i + 1) * TILE, :] = cols[:, i].reshape(TILE, PW)

    sides[...] = right_sides[...]

    def column_pair(jp, carry):
        factor = right[pl.ds(pl.multiple_of(jp * 256, 256), 256), :]

        def row_pair(ip, carry):
            product = lax.dot_general(
                left[pl.ds(pl.multiple_of(ip * 256, 256), 256), :],
                factor,
                (((1,), (1,)), ((), ())),
                preferred_element_type=jnp.float32,
            )
            for a in range(2):
                for b in range(2):
                    i, j = ip * 2 + a, jp * 2 + b
                    left_at, right_at = meta[1, row + i], meta[1, col + j]
                    real = (i < rows_here) & (j < cols_here) & ((left_at >> 3) == (right_at >> 3))

                    @pl.when(real)
                    def _():
                        at = (left_at & 7, pl.ds(right_at & 7, TILE, 8), slice(None))
                        tiles[at] = tiles[at] - product[a * TILE:(a + 1) * TILE, b * TILE:(b + 1) * TILE]

            return carry

        return lax.fori_loop(0, (rows_here + 1) // 2, row_pair, carry)

    lax.fori_loop(0, (cols_here + 1) // 2, column_pair, 0)

    for t in range(count):
        @pl.when(((row_bits >> t) & 1) == 1)
        def _():
            send_tile(tiles, t).start()

    def side(j, carry):
        at = meta[1, col + j]
        product = jnp.dot(
            right[pl.ds(pl.multiple_of(j * TILE, TILE), TILE), :],
            partial[at >> 3],
            preferred_element_type=jnp.float32,
        )
        sides[at & 7] = sides[at & 7] - product
        return carry

    lax.fori_loop(0, cols_here, side, 0)
    last = pltpu.make_async_copy(sides, out_sides, side_sem)
    last.start()
    for t in range(count):
        send_tile(tiles, t).wait()
    last.wait()


def update(slots, meta, rows, cols, partial, target, right_sides):
    vmem = pl.BlockSpec(memory_space=pltpu.VMEM)
    hbm = pl.BlockSpec(memory_space=pltpu.MemorySpace.HBM)
    return pl.pallas_call(
        functools.partial(update_kernel, slots),
        out_shape=(
            jax.ShapeDtypeStruct(target.shape, jnp.float32),
            jax.ShapeDtypeStruct(right_sides.shape, jnp.float32),
        ),
        in_specs=[pl.BlockSpec(memory_space=pltpu.SMEM)] + [vmem] * 5,
        out_specs=(hbm, hbm),
        scratch_shapes=[
            pltpu.VMEM(target.shape, jnp.float32),
            pltpu.VMEM(right_sides.shape, jnp.float32),
            pltpu.VMEM((slots * TILE, PW), jnp.bfloat16),
            pltpu.VMEM((slots * TILE, PW), jnp.bfloat16),
            pltpu.SemaphoreType.DMA((8,)),
            pltpu.SemaphoreType.DMA,
        ],
        compiler_params=pltpu.CompilerParams(vmem_limit_bytes=30 << 20),
        name="update_blocks",
    )(meta, rows, cols, partial, target, right_sides)


def shards(target, panel_a, inv_factor, panel_rhs, panel_rows, right_sides):
    slots = 16
    rows, cols, partial, meta, near_target, near_sides = gather(
        slots,
        panel_rows,
        panel_a,
        inv_factor,
        panel_rhs,
        target.reshape(8, 1024, 128),
        right_sides.reshape(8, 128, 256),
    )
    new_target, new_sides = update(slots, meta, rows, cols, partial, near_target, near_sides)
    return new_target.reshape(target.shape), new_sides.reshape(right_sides.shape)


def solution(mesh):
    placed = (
        P(None, "row", None, None, "col", None),
        P(None, "col", None, None),
        P(),
        P(None, "col", None),
        P(),
        P(None, "col", None, None),
    )
    return jax.shard_map(
        shards,
        mesh=mesh,
        in_specs=placed,
        out_specs=(P(None, "row", None, None, "col", None), P(None, "col", None, None)),
        check_vma=False,
    )
```

```python
import functools

import jax
import jax.numpy as jnp
from jax import lax
from jax.experimental import pallas as pl
from jax.experimental.pallas import tpu as pltpu
from jax.sharding import PartitionSpec as P

MESH = pl.DeviceIdType.MESH
NX, NY, NZ = 4, 4, 8
NROW, NCOL = 16, 16
SLAB = 8
PW = 512
NRHS = 256
TILE = 128
ZERO_BLOCK = 64
NEAREST = (1, 7, 2, 6, 3, 5, 4)


def remote(src, dst, send_sem, recv_sem, device):
    return pltpu.make_async_remote_copy(
        src_ref=src, dst_ref=dst, send_sem=send_sem, recv_sem=recv_sem, device_id=device, device_id_type=MESH
    )


class Copies:
    def __init__(self):
        self.sent = []

    def start(self, ref, send_sem, recv_sem, device):
        copy = remote(ref, ref, send_sem, recv_sem, device)
        copy.start()
        self.sent.append(copy)

    def arrived(self, ref, send_sem, recv_sem, device):
        remote(ref, ref, send_sem, recv_sem, device).wait_recv()

    def finish(self):
        for copy in self.sent:
            copy.wait_send()


class ZGather:
    def __init__(self, copies, piece, place, send, recv, mate_send, mate_recv):
        self.copies, self.piece = copies, piece
        self.row, self.z, self.k = place
        self.send, self.recv = send, recv
        self.mate_send, self.mate_recv = mate_send, mate_recv
        self.mate = (self.row, self.z * 2 + 1 - self.k)

    def chip(self, distance):
        return lax.rem(self.z + distance + NZ, NZ)

    def begin(self):
        own = self.piece(self.z * 2 + self.k)
        for d in NEAREST:
            self.copies.start(own, self.send.at[d], self.recv.at[d], (self.row, self.chip(d) * 2 + self.k))
        self.copies.start(own, self.mate_send.at[0], self.mate_recv.at[0], self.mate)

    def collect(self):
        for d in NEAREST:
            ref = self.piece(self.chip(-d) * 2 + self.k)
            self.copies.arrived(ref, self.send.at[d], self.recv.at[d], (self.row, self.chip(d) * 2 + self.k))
            self.copies.start(ref, self.mate_send.at[d], self.mate_recv.at[d], self.mate)

    def end(self):
        for d in (0,) + NEAREST:
            ref = self.piece(self.chip(-d) * 2 + 1 - self.k)
            self.copies.arrived(ref, self.mate_send.at[d], self.mate_recv.at[d], self.mate)


class PlaneGather:
    def __init__(self, copies, cols, half, place, send1, recv1, send2, recv2):
        self.copies, self.cols, self.half = copies, cols, half
        self.x, self.y, self.col = place
        self.send1, self.recv1, self.send2, self.recv2 = send1, recv1, send2, recv2
        count = cols.shape[1] // 2
        self.count, self.lead = count, (count + 1) // 2

    def row(self, along, across):
        dx, dy = (along, across) if self.half == 0 else (across, along)
        return lax.rem(self.x + dx + NX, NX) * NY + lax.rem(self.y + dy + NY, NY)

    def device(self, along, across):
        return (self.row(along, across), self.col)

    def ref(self, along, across, part):
        start = self.half * self.count + (self.lead if part == 1 else 0)
        size = {None: self.count, 0: self.lead, 1: self.count - self.lead}[part]
        return self.cols.at[self.row(along, across), pl.ds(start, size)]

    def shift(self, item):
        return (0, -1, 1, 2, 2)[item]

    def part(self, item):
        return (None, None, None, 0, 1)[item]

    def across_send(self, item):
        for way in range(2):
            self.copies.start(
                self.ref(self.shift(item), 0, self.part(item)),
                self.send2.at[item, way, 0],
                self.recv2.at[item, way, 0],
                self.device(0, 1 if way == 0 else -1),
            )

    def begin(self):
        for way in range(2):
            self.copies.start(
                self.ref(0, 0, None), self.send1.at[way, 0], self.recv1.at[way, 0], self.device(1 if way == 0 else -1, 0)
            )
        self.across_send(0)

    def near(self, way):
        towards = 1 if way == 0 else -1
        self.copies.arrived(
            self.ref(-towards, 0, None), self.send1.at[way, 0], self.recv1.at[way, 0], self.device(towards, 0)
        )
        self.copies.start(
            self.ref(-towards, 0, way), self.send1.at[way, 1], self.recv1.at[way, 1], self.device(towards, 0)
        )
        self.across_send(1 + way)

    def far(self, way):
        towards = 1 if way == 0 else -1
        self.copies.arrived(
            self.ref(2, 0, way), self.send1.at[way, 1], self.recv1.at[way, 1], self.device(towards, 0)
        )
        self.across_send(3 + way)

    def across_near(self, item):
        for way in range(2):
            towards = 1 if way == 0 else -1
            self.copies.arrived(
                self.ref(self.shift(item), -towards, self.part(item)),
                self.send2.at[item, way, 0],
                self.recv2.at[item, way, 0],
                self.device(0, towards),
            )
            if item < 3 or item - 3 == way:
                self.copies.start(
                    self.ref(self.shift(item), -towards, way),
                    self.send2.at[item, way, 1],
                    self.recv2.at[item, way, 1],
                    self.device(0, towards),
                )

    def across_far(self, item):
        for way in range(2):
            if item < 3 or item - 3 == way:
                self.copies.arrived(
                    self.ref(self.shift(item), 2, way),
                    self.send2.at[item, way, 1],
                    self.recv2.at[item, way, 1],
                    self.device(0, 1 if way == 0 else -1),
                )


def class_tables(panel_rows):
    count = panel_rows.shape[1]
    shape = (count, count)
    down = lax.broadcasted_iota(jnp.int32, shape, 0)
    across = lax.broadcasted_iota(jnp.int32, shape, 1)
    lane = lax.broadcasted_iota(jnp.int32, (count, 256), 1)
    block = lax.broadcasted_iota(jnp.int32, (count, 256), 0)
    wide = [jnp.broadcast_to(panel_rows[q:q + 1], shape) for q in range(2)]
    tall = [jnp.sum(jnp.where(down == across, w, 0), axis=1, keepdims=True) for w in wide]
    place, info, total = ZERO_BLOCK, 0, 0
    for q in range(2):
        same = (tall[q] & 15) == (wide[q] & 15)
        rank = jnp.sum(jnp.where(same & (across < down), 1, 0), axis=1, keepdims=True)
        if q == 1:
            rank += jnp.sum(jnp.where((tall[1] & 15) == (wide[0] & 15), 1, 0), axis=1, keepdims=True)
        hit = jnp.broadcast_to((tall[q] & 15) * 16 + rank, lane.shape) == lane
        where_from = (block >> 1) * 4 + (block & 1) + q * 2
        place += jnp.sum(jnp.where(hit, where_from - ZERO_BLOCK, 0), axis=0, keepdims=True)
        spot = jnp.broadcast_to((tall[q] >> 4) + q * 8, lane.shape)
        info += jnp.sum(jnp.where(hit, spot, 0), axis=0, keepdims=True)
        member = jnp.broadcast_to(tall[q] & 15, lane.shape) == (lane >> 4)
        total += jnp.sum(jnp.where(member, 1, 0), axis=0, keepdims=True)
    most = jnp.broadcast_to(jnp.max(total, axis=1, keepdims=True), total.shape)
    return place, info, total, most


def gather_kernel(
    slots,
    positions_hbm, panel, inv_hbm, rhs, target, right_sides,
    rows, cols, partial, meta, target_copy, sides_copy,
    positions, slab, inv_factor, solved, picked, sides, table, local_sem,
    z1, z1_in, mate1, mate1_in, z2, z2_in, mate2, mate2_in,
    swap, swap_in, hand, hand_in, plane1, plane1_in, plane2, plane2_in,
):
    row = lax.axis_index("row")
    col = lax.axis_index("col")
    x, y = row // NY, lax.rem(row, NY)
    z, k = col // 2, lax.rem(col, 2)
    place = (row, z, k)
    mate = (row, z * 2 + 1 - k)

    def load(src, dst, n):
        copy = pltpu.make_async_copy(src, dst, local_sem.at[n])
        copy.start()
        return copy

    own_rows = pl.ds(pl.multiple_of(row * SLAB, SLAB), SLAB)
    first = [load(panel.at[q, b, own_rows], slab.at[q, b], 2 * q + b) for q in range(2) for b in range(2)]
    first += [load(inv_hbm, inv_factor, 4)]
    second = [load(rhs, sides.at[col], 5), load(positions_hbm, positions, 9)]

    barrier = pltpu.get_barrier_semaphore()
    partners = [(row, lax.rem(z + d, NZ) * 2 + k) for d in NEAREST] + [mate]
    partners += [(lax.rem(row + d, NROW), col) for d in range(1, NROW)]
    for partner in partners:
        pl.semaphore_signal(barrier, inc=1, device_id=partner, device_id_type=MESH)

    solved[ZERO_BLOCK] = jnp.zeros((SLAB, PW), jnp.bfloat16)
    for copy in first:
        copy.wait()
    for q in range(2):
        block = slab[q].astype(jnp.float32).reshape(2 * SLAB, PW).astype(jnp.bfloat16)
        value = lax.dot_general(
            block, inv_factor[q], (((1,), (1,)), ((), ())), preferred_element_type=jnp.float32
        )
        for b in range(2):
            solved[col * 4 + q * 2 + b] = value[b * SLAB:(b + 1) * SLAB].astype(jnp.bfloat16)
    for copy in second:
        copy.wait()

    pl.semaphore_wait(barrier, len(partners))

    copies = Copies()
    slabs = ZGather(
        copies, lambda origin: solved.at[pl.ds(origin * 4, 4)], place, z1, z1_in, mate1, mate1_in
    )
    side_parts = ZGather(copies, lambda origin: sides.at[origin], place, z2, z2_in, mate2, mate2_in)
    planes = [
        PlaneGather(
            copies, cols, half, (x, y, col), plane1.at[half], plane1_in.at[half], plane2.at[half], plane2_in.at[half]
        )
        for half in range(2)
    ]

    slabs.begin()
    side_parts.begin()
    late = [load(target, target_copy, 6), load(right_sides, sides_copy, 7)]
    for n, values in enumerate(class_tables(positions[...])):
        meta[n:n + 1, :] = values
    to_scalars = load(meta, table, 8)
    to_scalars.wait()
    slabs.collect()
    slabs.end()

    for slot in range(slots):
        cols[row, slot] = solved[table[0, col * 16 + slot]]
    for plane in planes:
        plane.begin()

    share = slots // 2
    own_share = pl.ds(k * share, share)

    def send_picked(d, carry):
        there = lax.rem(row + d, NROW)
        for j in range(share):
            picked[d, j] = solved[table[0, there * 16 + k * share + j]]
        remote(picked.at[d], rows.at[row, own_share], swap.at[d], swap_in.at[d], (there, col)).start()
        return carry

    lax.fori_loop(1, NROW, send_picked, 0)
    for j in range(share):
        rows[row, k * share + j] = solved[table[0, row * 16 + k * share + j]]

    def hand_over(origin, d):
        ref = rows.at[origin, own_share]
        remote(ref, ref, hand.at[d], hand_in.at[d], mate).start()

    def receive_picked(d, carry):
        origin = lax.rem(row + NROW - d, NROW)
        ref = rows.at[origin, own_share]
        remote(picked.at[d], ref, swap.at[d], swap_in.at[d], (lax.rem(row + d, NROW), col)).wait()
        hand_over(origin, d)
        return carry

    hand_over(row, 0)
    for plane in planes:
        plane.near(0)
        plane.near(1)
    side_parts.collect()
    for plane in planes:
        plane.across_near(0)
    for plane in planes:
        plane.far(0)
        plane.far(1)
    for plane in planes:
        plane.across_near(1)
        plane.across_near(2)
    lax.fori_loop(1, NROW, receive_picked, 0)
    for plane in planes:
        plane.across_near(3)
        plane.across_near(4)
    side_parts.end()
    for q in range(2):
        value = jnp.dot(
            inv_factor[q], sides[:, q].reshape(PW, NRHS), preferred_element_type=jnp.float32
        )
        partial[q] = value.astype(jnp.bfloat16)

    def take_over(d, carry):
        origin = lax.rem(row + NROW - d, NROW)
        ref = rows.at[origin, pl.ds((1 - k) * share, share)]
        remote(ref, ref, hand.at[d], hand_in.at[d], mate).wait()
        return carry

    lax.fori_loop(0, NROW, take_over, 0)
    for item in range(5):
        for plane in planes:
            plane.across_far(item)
    for copy in late:
        copy.wait()
    copies.finish()


def gather(slots, number, panel_rows, panel, inv_factor, rhs, target, right_sides):
    dma = pltpu.SemaphoreType.DMA
    vmem = pl.BlockSpec(memory_space=pltpu.VMEM)
    hbm = pl.BlockSpec(memory_space=pltpu.MemorySpace.HBM)
    return pl.pallas_call(
        functools.partial(gather_kernel, slots),
        out_shape=(
            jax.ShapeDtypeStruct((NROW, slots, SLAB, PW), jnp.bfloat16),
            jax.ShapeDtypeStruct((NROW, slots, SLAB, PW), jnp.bfloat16),
            jax.ShapeDtypeStruct((2, PW, NRHS), jnp.bfloat16),
            jax.ShapeDtypeStruct((8, 256), jnp.int32),
            jax.ShapeDtypeStruct(target.shape, jnp.float32),
            jax.ShapeDtypeStruct(right_sides.shape, jnp.float32),
        ),
        in_specs=[hbm] * 6,
        out_specs=(vmem,) * 6,
        scratch_shapes=[
            pltpu.VMEM(panel_rows.shape, jnp.int32),
            pltpu.VMEM((2, 2, SLAB, PW), jnp.bfloat16),
            pltpu.VMEM((2, PW, PW), jnp.bfloat16),
            pltpu.VMEM((ZERO_BLOCK + 1, SLAB, PW), jnp.bfloat16),
            pltpu.VMEM((NROW, slots // 2, SLAB, PW), jnp.bfloat16),
            pltpu.VMEM((NCOL,) + rhs.shape, jnp.bfloat16),
            pltpu.SMEM((8, 256), jnp.int32),
            dma((10,)),
            dma((8,)), dma((8,)), dma((8,)), dma((8,)),
            dma((8,)), dma((8,)), dma((8,)), dma((8,)),
            dma((16,)), dma((16,)), dma((16,)), dma((16,)),
            dma((2, 2, 2)), dma((2, 2, 2)), dma((2, 5, 2, 2)), dma((2, 5, 2, 2)),
        ],
        compiler_params=pltpu.CompilerParams(
            collective_id=number, has_side_effects=True, vmem_limit_bytes=24 << 20
        ),
        name="gather_blocks",
    )(
        *[
            pltpu.with_memory_space_constraint(array, pltpu.MemorySpace.HBM)
            for array in (panel_rows, panel, inv_factor, rhs, target, right_sides)
        ]
    )


def update_kernel(
    slots,
    meta, rows, cols, partial, target, right_sides,
    out_target, out_sides,
    tiles, sides, left, right, product, tile_sem, side_sem,
):
    row = lax.axis_index("row") * 16
    col = lax.axis_index("col") * 16
    rows_here = meta[2, row]
    cols_here = meta[2, col]
    count = target.shape[0]

    def touched(base, total):
        bits = jnp.int32(0)
        for i in range(slots):
            bits |= jnp.where(i < total, jnp.int32(1) << (meta[1, base + i] & 7), 0)
        return bits

    row_bits = touched(row, rows_here)

    def send_tile(source, t):
        return pltpu.make_async_copy(source.at[t], out_target.at[t], tile_sem.at[t])

    for t in range(count):
        @pl.when(((row_bits >> t) & 1) == 0)
        def _():
            send_tile(target, t).start()

        @pl.when(((row_bits >> t) & 1) == 1)
        def _():
            tiles[t] = target[t]

    for i in range(slots):
        @pl.when(i < ((rows_here + 1) // 2) * 2)
        def _():
            left[i * TILE:(i + 1) * TILE, :] = rows[:, i].reshape(TILE, PW)

        @pl.when(i < ((cols_here + 1) // 2) * 2)
        def _():
            right[i * TILE:(i + 1) * TILE, :] = cols[:, i].reshape(TILE, PW)

    sides[...] = right_sides[...]

    half = slots // 2

    def column_pair(jp, carry):
        factor = right[pl.ds(pl.multiple_of(jp * 256, 256), 256), :]
        for part in range(2):
            @pl.when(part * half < rows_here)
            def _():
                product[...] = lax.dot_general(
                    left[part * half * TILE:(part + 1) * half * TILE, :],
                    factor,
                    (((1,), (1,)), ((), ())),
                    preferred_element_type=jnp.float32,
                )

                def subtract(i, carry):
                    left_at = meta[1, row + part * half + i]
                    for b in range(2):
                        right_at = meta[1, col + jp * 2 + b]

                        @pl.when((jp * 2 + b < cols_here) & ((left_at >> 3) == (right_at >> 3)))
                        def _():
                            at = (left_at & 7, pl.ds(right_at & 7, TILE, 8), slice(None))
                            block = product[pl.ds(pl.multiple_of(i * TILE, TILE), TILE), b * TILE:(b + 1) * TILE]
                            tiles[at] = tiles[at] - block

                    return carry

                lax.fori_loop(0, jnp.minimum(rows_here - part * half, half), subtract, 0)

        return carry

    lax.fori_loop(0, (cols_here + 1) // 2, column_pair, 0)

    for t in range(count):
        @pl.when(((row_bits >> t) & 1) == 1)
        def _():
            send_tile(tiles, t).start()

    def side(j, carry):
        at = meta[1, col + j]
        product = jnp.dot(
            right[pl.ds(pl.multiple_of(j * TILE, TILE), TILE), :],
            partial[at >> 3],
            preferred_element_type=jnp.float32,
        )
        sides[at & 7] = sides[at & 7] - product
        return carry

    lax.fori_loop(0, cols_here, side, 0)
    last = pltpu.make_async_copy(sides, out_sides, side_sem)
    last.start()
    for t in range(count):
        send_tile(tiles, t).wait()
    last.wait()


def update(slots, meta, rows, cols, partial, target, right_sides):
    vmem = pl.BlockSpec(memory_space=pltpu.VMEM)
    hbm = pl.BlockSpec(memory_space=pltpu.MemorySpace.HBM)
    return pl.pallas_call(
        functools.partial(update_kernel, slots),
        out_shape=(
            jax.ShapeDtypeStruct(target.shape, jnp.float32),
            jax.ShapeDtypeStruct(right_sides.shape, jnp.float32),
        ),
        in_specs=[pl.BlockSpec(memory_space=pltpu.SMEM)] + [vmem] * 5,
        out_specs=(hbm, hbm),
        scratch_shapes=[
            pltpu.VMEM(target.shape, jnp.float32),
            pltpu.VMEM(right_sides.shape, jnp.float32),
            pltpu.VMEM((slots * TILE, PW), jnp.bfloat16),
            pltpu.VMEM((slots * TILE, PW), jnp.bfloat16),
            pltpu.VMEM((slots // 2 * TILE, 2 * TILE), jnp.float32),
            pltpu.SemaphoreType.DMA((8,)),
            pltpu.SemaphoreType.DMA,
        ],
        compiler_params=pltpu.CompilerParams(vmem_limit_bytes=30 << 20),
        name="update_blocks",
    )(meta, rows, cols, partial, target, right_sides)


def shards(target, panel_a, inv_factor, panel_rhs, panel_rows, right_sides):
    few, most = 10, 16
    args = (panel_rows, panel_a, inv_factor, panel_rhs, target.reshape(8, 1024, 128), right_sides.reshape(8, 128, 256))
    rows, cols, partial, meta, near_target, near_sides = gather(few, 0, *args)

    def usual():
        return update(few, meta, rows, cols, partial, near_target, near_sides)

    def crowded():
        rows, cols, partial, meta, near_target, near_sides = gather(most, 1, *args)
        return update(most, meta, rows, cols, partial, near_target, near_sides)

    new_target, new_sides = lax.cond(meta[3, 0] <= few, usual, crowded)
    return new_target.reshape(target.shape), new_sides.reshape(right_sides.shape)


def solution(mesh):
    placed = (
        P(None, "row", None, None, "col", None),
        P(None, "col", None, None),
        P(),
        P(None, "col", None),
        P(),
        P(None, "col", None, None),
    )
    return jax.shard_map(
        shards,
        mesh=mesh,
        in_specs=placed,
        out_specs=(P(None, "row", None, None, "col", None), P(None, "col", None, None)),
        check_vma=False,
    )
```

```python
import functools

import jax
import jax.numpy as jnp
from jax import lax
from jax.experimental import pallas as pl
from jax.experimental.pallas import tpu as pltpu
from jax.sharding import PartitionSpec as P

MESH = pl.DeviceIdType.MESH
NX, NY, NZ = 4, 4, 8
NROW, NCOL = 16, 16
SLAB = 8
PW = 512
NRHS = 256
TILE = 128
ZERO_BLOCK = 64
NEAREST = (1, 7, 2, 6, 3, 5, 4)


def remote(src, dst, send_sem, recv_sem, device):
    return pltpu.make_async_remote_copy(
        src_ref=src, dst_ref=dst, send_sem=send_sem, recv_sem=recv_sem, device_id=device, device_id_type=MESH
    )


class Copies:
    def __init__(self):
        self.sent = []

    def start(self, ref, send_sem, recv_sem, device):
        copy = remote(ref, ref, send_sem, recv_sem, device)
        copy.start()
        self.sent.append(copy)

    def arrived(self, ref, send_sem, recv_sem, device):
        remote(ref, ref, send_sem, recv_sem, device).wait_recv()

    def finish(self):
        for copy in self.sent:
            copy.wait_send()


class ZGather:
    def __init__(self, copies, piece, place, send, recv, mate_send, mate_recv):
        self.copies, self.piece = copies, piece
        self.row, self.z, self.k = place
        self.send, self.recv = send, recv
        self.mate_send, self.mate_recv = mate_send, mate_recv
        self.mate = (self.row, self.z * 2 + 1 - self.k)

    def chip(self, distance):
        return lax.rem(self.z + distance + NZ, NZ)

    def begin(self):
        own = self.piece(self.z * 2 + self.k)
        for d in NEAREST:
            self.copies.start(own, self.send.at[d], self.recv.at[d], (self.row, self.chip(d) * 2 + self.k))
        self.copies.start(own, self.mate_send.at[0], self.mate_recv.at[0], self.mate)

    def collect(self):
        for d in NEAREST:
            ref = self.piece(self.chip(-d) * 2 + self.k)
            self.copies.arrived(ref, self.send.at[d], self.recv.at[d], (self.row, self.chip(d) * 2 + self.k))
            self.copies.start(ref, self.mate_send.at[d], self.mate_recv.at[d], self.mate)

    def end(self):
        for d in (0,) + NEAREST:
            ref = self.piece(self.chip(-d) * 2 + 1 - self.k)
            self.copies.arrived(ref, self.mate_send.at[d], self.mate_recv.at[d], self.mate)


class PlaneGather:
    def __init__(self, copies, cols, half, place, send1, recv1, send2, recv2):
        self.copies, self.cols, self.half = copies, cols, half
        self.x, self.y, self.col = place
        self.send1, self.recv1, self.send2, self.recv2 = send1, recv1, send2, recv2
        count = cols.shape[1] // 2
        self.count, self.lead = count, (count + 1) // 2

    def row(self, along, across):
        dx, dy = (along, across) if self.half == 0 else (across, along)
        return lax.rem(self.x + dx + NX, NX) * NY + lax.rem(self.y + dy + NY, NY)

    def device(self, along, across):
        return (self.row(along, across), self.col)

    def ref(self, along, across, part):
        start = self.half * self.count + (self.lead if part == 1 else 0)
        size = {None: self.count, 0: self.lead, 1: self.count - self.lead}[part]
        return self.cols.at[self.row(along, across), pl.ds(start, size)]

    def shift(self, item):
        return (0, -1, 1, 2, 2)[item]

    def part(self, item):
        return (None, None, None, 0, 1)[item]

    def across_send(self, item):
        for way in range(2):
            self.copies.start(
                self.ref(self.shift(item), 0, self.part(item)),
                self.send2.at[item, way, 0],
                self.recv2.at[item, way, 0],
                self.device(0, 1 if way == 0 else -1),
            )

    def begin(self):
        for way in range(2):
            self.copies.start(
                self.ref(0, 0, None), self.send1.at[way, 0], self.recv1.at[way, 0], self.device(1 if way == 0 else -1, 0)
            )
        self.across_send(0)

    def near(self, way):
        towards = 1 if way == 0 else -1
        self.copies.arrived(
            self.ref(-towards, 0, None), self.send1.at[way, 0], self.recv1.at[way, 0], self.device(towards, 0)
        )
        self.copies.start(
            self.ref(-towards, 0, way), self.send1.at[way, 1], self.recv1.at[way, 1], self.device(towards, 0)
        )
        self.across_send(1 + way)

    def far(self, way):
        towards = 1 if way == 0 else -1
        self.copies.arrived(
            self.ref(2, 0, way), self.send1.at[way, 1], self.recv1.at[way, 1], self.device(towards, 0)
        )
        self.across_send(3 + way)

    def across_near(self, item):
        for way in range(2):
            towards = 1 if way == 0 else -1
            self.copies.arrived(
                self.ref(self.shift(item), -towards, self.part(item)),
                self.send2.at[item, way, 0],
                self.recv2.at[item, way, 0],
                self.device(0, towards),
            )
            if item < 3 or item - 3 == way:
                self.copies.start(
                    self.ref(self.shift(item), -towards, way),
                    self.send2.at[item, way, 1],
                    self.recv2.at[item, way, 1],
                    self.device(0, towards),
                )

    def across_far(self, item):
        for way in range(2):
            if item < 3 or item - 3 == way:
                self.copies.arrived(
                    self.ref(self.shift(item), 2, way),
                    self.send2.at[item, way, 1],
                    self.recv2.at[item, way, 1],
                    self.device(0, 1 if way == 0 else -1),
                )


def class_tables(panel_rows):
    count = panel_rows.shape[1]
    shape = (count, count)
    down = lax.broadcasted_iota(jnp.int32, shape, 0)
    across = lax.broadcasted_iota(jnp.int32, shape, 1)
    lane = lax.broadcasted_iota(jnp.int32, (count, 256), 1)
    block = lax.broadcasted_iota(jnp.int32, (count, 256), 0)
    wide = [jnp.broadcast_to(panel_rows[q:q + 1], shape) for q in range(2)]
    tall = [jnp.sum(jnp.where(down == across, w, 0), axis=1, keepdims=True) for w in wide]
    place, info, total = ZERO_BLOCK, 0, 0
    for q in range(2):
        same = (tall[q] & 15) == (wide[q] & 15)
        rank = jnp.sum(jnp.where(same & (across < down), 1, 0), axis=1, keepdims=True)
        if q == 1:
            rank += jnp.sum(jnp.where((tall[1] & 15) == (wide[0] & 15), 1, 0), axis=1, keepdims=True)
        hit = jnp.broadcast_to((tall[q] & 15) * 16 + rank, lane.shape) == lane
        where_from = (block >> 1) * 4 + (block & 1) + q * 2
        place += jnp.sum(jnp.where(hit, where_from - ZERO_BLOCK, 0), axis=0, keepdims=True)
        spot = jnp.broadcast_to((tall[q] >> 4) + q * 8, lane.shape)
        info += jnp.sum(jnp.where(hit, spot, 0), axis=0, keepdims=True)
        member = jnp.broadcast_to(tall[q] & 15, lane.shape) == (lane >> 4)
        total += jnp.sum(jnp.where(member, 1, 0), axis=0, keepdims=True)
        if q == 0:
            lead = total
    most = jnp.broadcast_to(jnp.max(total, axis=1, keepdims=True), total.shape)
    return place, info, total, most, lead


def gather_kernel(
    slots,
    positions_hbm, panel, inv_hbm, rhs, target, right_sides,
    rows, cols, partial, meta, target_copy, sides_copy,
    positions, slab, inv_factor, solved, picked, sides, table, local_sem,
    z1, z1_in, mate1, mate1_in, z2, z2_in, mate2, mate2_in,
    swap, swap_in, climb, climb_in, hand, hand_in, plane1, plane1_in, plane2, plane2_in,
):
    row = lax.axis_index("row")
    col = lax.axis_index("col")
    x, y = row // NY, lax.rem(row, NY)
    z, k = col // 2, lax.rem(col, 2)
    place = (row, z, k)
    mate = (row, z * 2 + 1 - k)

    def load(src, dst, n):
        copy = pltpu.make_async_copy(src, dst, local_sem.at[n])
        copy.start()
        return copy

    own_rows = pl.ds(pl.multiple_of(row * SLAB, SLAB), SLAB)
    first = [load(panel.at[q, b, own_rows], slab.at[q, b], 2 * q + b) for q in range(2) for b in range(2)]
    first += [load(inv_hbm, inv_factor, 4)]
    second = [load(rhs, sides.at[col], 5), load(positions_hbm, positions, 9)]

    barrier = pltpu.get_barrier_semaphore()
    partners = [(row, lax.rem(z + d, NZ) * 2 + k) for d in NEAREST] + [mate]
    partners += [(lax.rem(row + d, NROW), col) for d in range(1, NROW)]
    for partner in partners:
        pl.semaphore_signal(barrier, inc=1, device_id=partner, device_id_type=MESH)

    solved[ZERO_BLOCK] = jnp.zeros((SLAB, PW), jnp.bfloat16)
    for copy in first:
        copy.wait()
    for q in range(2):
        block = slab[q].astype(jnp.float32).reshape(2 * SLAB, PW).astype(jnp.bfloat16)
        value = lax.dot_general(
            block, inv_factor[q], (((1,), (1,)), ((), ())), preferred_element_type=jnp.float32
        )
        for b in range(2):
            solved[col * 4 + q * 2 + b] = value[b * SLAB:(b + 1) * SLAB].astype(jnp.bfloat16)
    for copy in second:
        copy.wait()

    pl.semaphore_wait(barrier, len(partners))

    copies = Copies()
    slabs = ZGather(
        copies, lambda origin: solved.at[pl.ds(origin * 4, 4)], place, z1, z1_in, mate1, mate1_in
    )
    side_parts = ZGather(copies, lambda origin: sides.at[origin], place, z2, z2_in, mate2, mate2_in)
    planes = [
        PlaneGather(
            copies, cols, half, (x, y, col), plane1.at[half], plane1_in.at[half], plane2.at[half], plane2_in.at[half]
        )
        for half in range(2)
    ]

    slabs.begin()
    late = [load(target, target_copy, 6), load(right_sides, sides_copy, 7)]
    for n, values in enumerate(class_tables(positions[...])):
        meta[n:n + 1, :] = values
    to_scalars = load(meta, table, 8)
    to_scalars.wait()
    slabs.collect()
    slabs.end()

    share = slots // 2
    width = PW // 2
    mine = pl.ds(pl.multiple_of(k * width, width), width)
    theirs = pl.ds(pl.multiple_of((1 - k) * width, width), width)
    here = lax.rem(z, 2) * share
    above = (row, lax.rem(z + 1, NZ) * 2 + k)
    below = (row, lax.rem(z + NZ - 1, NZ) * 2 + k)

    def row_piece(slab_index, start, columns):
        return rows.at[slab_index, pl.ds(start, share), :, columns]

    def send_rows(d, carry):
        there = lax.rem(row + d, NROW)
        for j in range(share):
            picked[d, j] = solved[table[0, there * 16 + here + j], :, mine]
        remote(picked.at[d], row_piece(row, here, mine), swap.at[d], swap_in.at[d], (there, col)).start()
        return carry

    def pass_rows(origin):
        ref = row_piece(origin, here, mine)
        remote(ref, ref, hand.at[0, origin], hand_in.at[0, origin], mate).start()

        @pl.when(origin < NROW // 2)
        def _():
            remote(ref, ref, climb.at[origin], climb_in.at[origin], above).start()

        @pl.when(origin >= NROW // 2)
        def _():
            remote(ref, ref, climb.at[origin], climb_in.at[origin], below).start()

    def receive_rows(d, carry):
        origin = lax.rem(row + NROW - d, NROW)
        ref = row_piece(origin, here, mine)
        remote(picked.at[d], ref, swap.at[d], swap_in.at[d], (lax.rem(row + d, NROW), col)).wait()
        pass_rows(origin)
        return carry

    def receive_climbed(n, carry):
        ref = row_piece(n, share - here, mine)
        remote(ref, ref, climb.at[n], climb_in.at[n], above).wait()
        remote(ref, ref, hand.at[1, n], hand_in.at[1, n], mate).start()
        return carry

    def take_over(n, carry):
        for which, start in ((0, here), (1, share - here)):
            ref = row_piece(n, start, theirs)
            remote(ref, ref, hand.at[which, n], hand_in.at[which, n], mate).wait()
        return carry

    lax.fori_loop(1, NROW, send_rows, 0)
    for slot in range(slots):
        cols[row, slot] = solved[table[0, col * 16 + slot]]
    for plane in planes:
        plane.begin()
    for j in range(share):
        rows[row, here + j, :, mine] = solved[table[0, row * 16 + here + j], :, mine]
    pass_rows(row)
    side_parts.begin()
    for plane in planes:
        plane.near(0)
        plane.near(1)
    lax.fori_loop(1, NROW, receive_rows, 0)
    for plane in planes:
        plane.across_near(0)
    for plane in planes:
        plane.far(0)
        plane.far(1)
    side_parts.collect()
    for plane in planes:
        plane.across_near(1)
        plane.across_near(2)
    lax.fori_loop(0, NROW, receive_climbed, 0)
    for plane in planes:
        plane.across_near(3)
        plane.across_near(4)
    side_parts.end()
    for q in range(2):
        value = jnp.dot(
            inv_factor[q], sides[:, q].reshape(PW, NRHS), preferred_element_type=jnp.float32
        )
        partial[q] = value.astype(jnp.bfloat16)
    lax.fori_loop(0, NROW, take_over, 0)
    for item in range(5):
        for plane in planes:
            plane.across_far(item)
    for copy in late:
        copy.wait()
    copies.finish()


def gather(slots, number, panel_rows, panel, inv_factor, rhs, target, right_sides):
    dma = pltpu.SemaphoreType.DMA
    vmem = pl.BlockSpec(memory_space=pltpu.VMEM)
    hbm = pl.BlockSpec(memory_space=pltpu.MemorySpace.HBM)
    return pl.pallas_call(
        functools.partial(gather_kernel, slots),
        out_shape=(
            jax.ShapeDtypeStruct((NROW, slots, SLAB, PW), jnp.bfloat16),
            jax.ShapeDtypeStruct((NROW, slots, SLAB, PW), jnp.bfloat16),
            jax.ShapeDtypeStruct((2, PW, NRHS), jnp.bfloat16),
            jax.ShapeDtypeStruct((8, 256), jnp.int32),
            jax.ShapeDtypeStruct(target.shape, jnp.float32),
            jax.ShapeDtypeStruct(right_sides.shape, jnp.float32),
        ),
        in_specs=[hbm] * 6,
        out_specs=(vmem,) * 6,
        scratch_shapes=[
            pltpu.VMEM(panel_rows.shape, jnp.int32),
            pltpu.VMEM((2, 2, SLAB, PW), jnp.bfloat16),
            pltpu.VMEM((2, PW, PW), jnp.bfloat16),
            pltpu.VMEM((ZERO_BLOCK + 1, SLAB, PW), jnp.bfloat16),
            pltpu.VMEM((NROW, slots // 2, SLAB, PW // 2), jnp.bfloat16),
            pltpu.VMEM((NCOL,) + rhs.shape, jnp.bfloat16),
            pltpu.SMEM((8, 256), jnp.int32),
            dma((10,)),
            dma((8,)), dma((8,)), dma((8,)), dma((8,)),
            dma((8,)), dma((8,)), dma((8,)), dma((8,)),
            dma((16,)), dma((16,)), dma((16,)), dma((16,)), dma((2, 16)), dma((2, 16)),
            dma((2, 2, 2)), dma((2, 2, 2)), dma((2, 5, 2, 2)), dma((2, 5, 2, 2)),
        ],
        compiler_params=pltpu.CompilerParams(
            collective_id=number, has_side_effects=True, vmem_limit_bytes=24 << 20
        ),
        name="gather_blocks",
    )(
        *[
            pltpu.with_memory_space_constraint(array, pltpu.MemorySpace.HBM)
            for array in (panel_rows, panel, inv_factor, rhs, target, right_sides)
        ]
    )


def update_kernel(
    slots,
    meta, rows, cols, partial, target, right_sides,
    out_target, out_sides,
    tiles, sides, left, right, product, tile_sem, side_sem,
):
    row = lax.axis_index("row") * 16
    col = lax.axis_index("col") * 16
    rows_here = meta[2, row]
    cols_here = meta[2, col]
    count = target.shape[0]

    def touched(base, total):
        bits = jnp.int32(0)
        for i in range(slots):
            bits |= jnp.where(i < total, jnp.int32(1) << (meta[1, base + i] & 7), 0)
        return bits

    row_bits = touched(row, rows_here)

    def send_tile(source, t):
        return pltpu.make_async_copy(source.at[t], out_target.at[t], tile_sem.at[t])

    for t in range(count):
        @pl.when(((row_bits >> t) & 1) == 0)
        def _():
            send_tile(target, t).start()

        @pl.when(((row_bits >> t) & 1) == 1)
        def _():
            tiles[t] = target[t]

    for i in range(slots):
        @pl.when(i < rows_here)
        def _():
            left[i * TILE:(i + 1) * TILE, :] = rows[:, i].reshape(TILE, PW)

        @pl.when(i < cols_here)
        def _():
            right[i * TILE:(i + 1) * TILE, :] = cols[:, i].reshape(TILE, PW)

    sides[...] = right_sides[...]

    half = slots // 2
    row_split, col_split = meta[4, row], meta[4, col]

    for q in range(2):
        row_from, row_to = (0, row_split) if q == 0 else (row_split, rows_here)
        col_from, col_to = (0, col_split) if q == 0 else (col_split, cols_here)

        def column_pair(jp, carry):
            j = col_from + jp * 2
            factor = right[pl.ds(pl.multiple_of(j * TILE, TILE), 2 * TILE), :]

            def row_group(part, carry):
                start = row_from + part * half
                product[...] = lax.dot_general(
                    left[pl.ds(pl.multiple_of(start * TILE, TILE), half * TILE), :],
                    factor,
                    (((1,), (1,)), ((), ())),
                    preferred_element_type=jnp.float32,
                )

                def subtract(i, carry):
                    t = meta[1, row + start + i] & 7
                    for b in range(2):
                        @pl.when(j + b < col_to)
                        def _():
                            at = (t, pl.ds(meta[1, col + j + b] & 7, TILE, 8), slice(None))
                            block = product[pl.ds(pl.multiple_of(i * TILE, TILE), TILE), b * TILE:(b + 1) * TILE]
                            tiles[at] = tiles[at] - block

                    return carry

                return lax.fori_loop(0, jnp.minimum(row_to - start, half), subtract, carry)

            return lax.fori_loop(0, (row_to - row_from + half - 1) // half, row_group, carry)

        lax.fori_loop(0, (col_to - col_from + 1) // 2, column_pair, 0)

    for t in range(count):
        @pl.when(((row_bits >> t) & 1) == 1)
        def _():
            send_tile(tiles, t).start()

    def side(j, carry):
        at = meta[1, col + j]
        product = jnp.dot(
            right[pl.ds(pl.multiple_of(j * TILE, TILE), TILE), :],
            partial[at >> 3],
            preferred_element_type=jnp.float32,
        )
        sides[at & 7] = sides[at & 7] - product
        return carry

    lax.fori_loop(0, cols_here, side, 0)
    last = pltpu.make_async_copy(sides, out_sides, side_sem)
    last.start()
    for t in range(count):
        send_tile(tiles, t).wait()
    last.wait()


def update(slots, meta, rows, cols, partial, target, right_sides):
    vmem = pl.BlockSpec(memory_space=pltpu.VMEM)
    hbm = pl.BlockSpec(memory_space=pltpu.MemorySpace.HBM)
    return pl.pallas_call(
        functools.partial(update_kernel, slots),
        out_shape=(
            jax.ShapeDtypeStruct(target.shape, jnp.float32),
            jax.ShapeDtypeStruct(right_sides.shape, jnp.float32),
        ),
        in_specs=[pl.BlockSpec(memory_space=pltpu.SMEM)] + [vmem] * 5,
        out_specs=(hbm, hbm),
        scratch_shapes=[
            pltpu.VMEM(target.shape, jnp.float32),
            pltpu.VMEM(right_sides.shape, jnp.float32),
            pltpu.VMEM(((slots + slots // 2) * TILE, PW), jnp.bfloat16),
            pltpu.VMEM(((slots + 1) * TILE, PW), jnp.bfloat16),
            pltpu.VMEM((slots // 2 * TILE, 2 * TILE), jnp.float32),
            pltpu.SemaphoreType.DMA((8,)),
            pltpu.SemaphoreType.DMA,
        ],
        compiler_params=pltpu.CompilerParams(vmem_limit_bytes=30 << 20),
        name="update_blocks",
    )(meta, rows, cols, partial, target, right_sides)


def shards(target, panel_a, inv_factor, panel_rhs, panel_rows, right_sides):
    few, most = 10, 16
    args = (panel_rows, panel_a, inv_factor, panel_rhs, target.reshape(8, 1024, 128), right_sides.reshape(8, 128, 256))
    rows, cols, partial, meta, near_target, near_sides = gather(few, 0, *args)

    def usual():
        return update(few, meta, rows, cols, partial, near_target, near_sides)

    def crowded():
        rows, cols, partial, meta, near_target, near_sides = gather(most, 1, *args)
        return update(most, meta, rows, cols, partial, near_target, near_sides)

    new_target, new_sides = lax.cond(meta[3, 0] <= few, usual, crowded)
    return new_target.reshape(target.shape), new_sides.reshape(right_sides.shape)


def solution(mesh):
    placed = (
        P(None, "row", None, None, "col", None),
        P(None, "col", None, None),
        P(),
        P(None, "col", None),
        P(),
        P(None, "col", None, None),
    )
    return jax.shard_map(
        shards,
        mesh=mesh,
        in_specs=placed,
        out_specs=(P(None, "row", None, None, "col", None), P(None, "col", None, None)),
        check_vma=False,
    )
```

```python
import functools

import jax
import jax.numpy as jnp
from jax import lax
from jax.experimental import pallas as pl
from jax.experimental.pallas import tpu as pltpu
from jax.sharding import PartitionSpec as P

MESH = pl.DeviceIdType.MESH
NX, NY, NZ = 4, 4, 8
NROW, NCOL = 16, 16
SLAB = 8
PW = 512
NRHS = 256
TILE = 128
ZERO_BLOCK = 64
NEAREST = (1, 7, 2, 6, 3, 5, 4)


def remote(src, dst, send_sem, recv_sem, device):
    return pltpu.make_async_remote_copy(
        src_ref=src, dst_ref=dst, send_sem=send_sem, recv_sem=recv_sem, device_id=device, device_id_type=MESH
    )


class Copies:
    def __init__(self):
        self.sent = []

    def start(self, ref, send_sem, recv_sem, device):
        copy = remote(ref, ref, send_sem, recv_sem, device)
        copy.start()
        self.sent.append(copy)

    def arrived(self, ref, send_sem, recv_sem, device):
        remote(ref, ref, send_sem, recv_sem, device).wait_recv()

    def finish(self):
        for copy in self.sent:
            copy.wait_send()
        self.sent = []


class ZGather:
    def __init__(self, copies, piece, place, send, recv, mate_send, mate_recv):
        self.copies, self.piece = copies, piece
        self.row, self.z, self.k = place
        self.send, self.recv = send, recv
        self.mate_send, self.mate_recv = mate_send, mate_recv
        self.mate = (self.row, self.z * 2 + 1 - self.k)

    def chip(self, distance):
        return lax.rem(self.z + distance + NZ, NZ)

    def begin(self):
        own = self.piece(self.z * 2 + self.k)
        for d in NEAREST:
            self.copies.start(own, self.send.at[d], self.recv.at[d], (self.row, self.chip(d) * 2 + self.k))
        self.copies.start(own, self.mate_send.at[0], self.mate_recv.at[0], self.mate)

    def collect(self):
        for d in NEAREST:
            ref = self.piece(self.chip(-d) * 2 + self.k)
            self.copies.arrived(ref, self.send.at[d], self.recv.at[d], (self.row, self.chip(d) * 2 + self.k))
            self.copies.start(ref, self.mate_send.at[d], self.mate_recv.at[d], self.mate)

    def end(self):
        for d in (0,) + NEAREST:
            ref = self.piece(self.chip(-d) * 2 + 1 - self.k)
            self.copies.arrived(ref, self.mate_send.at[d], self.mate_recv.at[d], self.mate)


class PlaneGather:
    def __init__(self, copies, cols, half, place, send1, recv1, send2, recv2):
        self.copies, self.cols, self.half = copies, cols, half
        self.x, self.y, self.col = place
        self.send1, self.recv1, self.send2, self.recv2 = send1, recv1, send2, recv2
        count = cols.shape[2] // 2
        self.slots = pl.ds(half * count, count)

    def move(self, stage, distance):
        along_x = (stage == 1) == (self.half == 0)
        x = lax.rem(self.x + distance + NX, NX) if along_x else self.x
        y = self.y if along_x else lax.rem(self.y + distance + NY, NY)
        return x, y

    def device(self, stage, distance):
        x, y = self.move(stage, distance)
        return (x * NY + y, self.col)

    def ref(self, stage, distance):
        x, y = self.move(stage, distance)
        if stage == 1:
            return self.cols.at[x, y, self.slots]
        return self.cols.at[:, y, self.slots] if self.half == 0 else self.cols.at[x, :, self.slots]

    def send(self, stage):
        sems = (self.send1, self.recv1) if stage == 1 else (self.send2, self.recv2)
        for d in (1, 3, 2):
            self.copies.start(self.ref(stage, 0), sems[0].at[d], sems[1].at[d], self.device(stage, d))

    def receive(self, stage):
        sems = (self.send1, self.recv1) if stage == 1 else (self.send2, self.recv2)
        for d in (1, 3, 2):
            self.copies.arrived(self.ref(stage, -d), sems[0].at[d], sems[1].at[d], self.device(stage, d))


def class_tables(panel_rows):
    count = panel_rows.shape[1]
    shape = (count, count)
    down = lax.broadcasted_iota(jnp.int32, shape, 0)
    across = lax.broadcasted_iota(jnp.int32, shape, 1)
    lane = lax.broadcasted_iota(jnp.int32, (count, 256), 1)
    block = lax.broadcasted_iota(jnp.int32, (count, 256), 0)
    wide = [jnp.broadcast_to(panel_rows[q:q + 1], shape) for q in range(2)]
    tall = [jnp.sum(jnp.where(down == across, w, 0), axis=1, keepdims=True) for w in wide]
    place, info, total = ZERO_BLOCK, 0, 0
    for q in range(2):
        same = (tall[q] & 15) == (wide[q] & 15)
        rank = jnp.sum(jnp.where(same & (across < down), 1, 0), axis=1, keepdims=True)
        if q == 1:
            rank += jnp.sum(jnp.where((tall[1] & 15) == (wide[0] & 15), 1, 0), axis=1, keepdims=True)
        hit = jnp.broadcast_to((tall[q] & 15) * 16 + rank, lane.shape) == lane
        where_from = (block >> 1) * 4 + (block & 1) + q * 2
        place += jnp.sum(jnp.where(hit, where_from - ZERO_BLOCK, 0), axis=0, keepdims=True)
        spot = jnp.broadcast_to((tall[q] >> 4) + q * 8, lane.shape)
        info += jnp.sum(jnp.where(hit, spot, 0), axis=0, keepdims=True)
        member = jnp.broadcast_to(tall[q] & 15, lane.shape) == (lane >> 4)
        total += jnp.sum(jnp.where(member, 1, 0), axis=0, keepdims=True)
        if q == 0:
            lead = total
    most = jnp.broadcast_to(jnp.max(total, axis=1, keepdims=True), total.shape)
    return place, info, total, most, lead


def gather_kernel(
    slots,
    positions_hbm, panel, inv_hbm, rhs, target, right_sides,
    rows, cols, partial, meta, target_copy, sides_copy,
    positions, slab, inv_factor, solved, picked, sides, table, local_sem, ready,
    z1, z1_in, mate1, mate1_in, z2, z2_in, mate2, mate2_in,
    swap, swap_in, climb, climb_in, hand, hand_in, plane1, plane1_in, plane2, plane2_in,
):
    row = lax.axis_index("row")
    col = lax.axis_index("col")
    x, y = row // NY, lax.rem(row, NY)
    z, k = col // 2, lax.rem(col, 2)
    place = (row, z, k)
    mate = (row, z * 2 + 1 - k)

    def load(src, dst, n):
        copy = pltpu.make_async_copy(src, dst, local_sem.at[n])
        copy.start()
        return copy

    own_rows = pl.ds(pl.multiple_of(row * SLAB, SLAB), SLAB)
    first = [load(panel.at[q, b, own_rows], slab.at[q, b], 2 * q + b) for q in range(2) for b in range(2)]
    first += [load(inv_hbm, inv_factor, 4)]
    second = [load(rhs, sides.at[k, z], 5), load(positions_hbm, positions, 9)]

    barrier = pltpu.get_barrier_semaphore()
    partners = [(row, lax.rem(z + d, NZ) * 2 + k) for d in NEAREST] + [mate]
    ring_x = [(lax.rem(x + d, NX) * NY + y, col) for d in range(1, NX)]
    ring_y = [(x * NY + lax.rem(y + d, NY), col) for d in range(1, NY)]
    partners += ring_x + ring_y
    for partner in partners:
        pl.semaphore_signal(barrier, inc=1, device_id=partner, device_id_type=MESH)

    solved[ZERO_BLOCK] = jnp.zeros((SLAB, PW), jnp.bfloat16)
    for copy in first:
        copy.wait()
    for q in range(2):
        block = slab[q].astype(jnp.float32).reshape(2 * SLAB, PW).astype(jnp.bfloat16)
        value = lax.dot_general(
            block, inv_factor[q], (((1,), (1,)), ((), ())), preferred_element_type=jnp.float32
        )
        for b in range(2):
            solved[col * 4 + q * 2 + b] = value[b * SLAB:(b + 1) * SLAB].astype(jnp.bfloat16)
    for copy in second:
        copy.wait()

    pl.semaphore_wait(barrier, len(partners))

    copies = Copies()
    slabs = ZGather(
        copies, lambda origin: solved.at[pl.ds(origin * 4, 4)], place, z1, z1_in, mate1, mate1_in
    )
    planes = [
        PlaneGather(
            copies, cols, half, (x, y, col), plane1.at[half], plane1_in.at[half], plane2.at[half], plane2_in.at[half]
        )
        for half in range(2)
    ]

    slabs.begin()
    for partner in ring_x:
        pl.semaphore_signal(ready, inc=1, device_id=partner, device_id_type=MESH)
    late = [load(target, target_copy, 6), load(right_sides, sides_copy, 7)]
    for n, values in enumerate(class_tables(positions[...])):
        meta[n:n + 1, :] = values
    to_scalars = load(meta, table, 8)
    to_scalars.wait()
    slabs.collect()
    slabs.end()
    pl.semaphore_wait(ready, len(ring_x))

    share = slots // 2
    width = PW // 2
    mine = pl.ds(pl.multiple_of(k * width, width), width)
    theirs = pl.ds(pl.multiple_of((1 - k) * width, width), width)
    here = lax.rem(z, 2) * share
    above = (row, lax.rem(z + 1, NZ) * 2 + k)
    below = (row, lax.rem(z + NZ - 1, NZ) * 2 + k)

    def row_piece(slabs_from, start, columns):
        return rows.at[slabs_from, pl.ds(start, share), :, columns]

    def send_rows(d, carry):
        there = lax.rem(row + d, NROW)
        for j in range(share):
            picked[d, j] = solved[table[0, there * 16 + here + j], :, mine]
        remote(picked.at[d], row_piece(row, here, mine), swap.at[d], swap_in.at[d], (there, col)).start()
        return carry

    every = pl.ds(0, NROW)
    lower, upper = pl.ds(0, NROW // 2), pl.ds(NROW // 2, NROW // 2)

    def receive_rows(d, carry):
        ref = row_piece(lax.rem(row + NROW - d, NROW), here, mine)
        remote(picked.at[d], ref, swap.at[d], swap_in.at[d], (lax.rem(row + d, NROW), col)).wait()
        return carry

    for slot in range(slots):
        cols[x, y, slot] = solved[table[0, col * 16 + slot]]
    for plane in planes:
        plane.send(1)
    lax.fori_loop(1, NROW, send_rows, 0)
    for j in range(share):
        rows[row, here + j, :, mine] = solved[table[0, row * 16 + here + j], :, mine]
    for d in NEAREST:
        copies.start(sides.at[k, z], z2.at[d], z2_in.at[d], (row, lax.rem(z + d, NZ) * 2 + k))
    for plane in planes:
        plane.receive(1)
    copies.finish()
    for plane in planes:
        plane.send(2)
    lax.fori_loop(1, NROW, receive_rows, 0)
    copies.start(row_piece(lower, here, mine), climb.at[0], climb_in.at[0], above)
    copies.start(row_piece(upper, here, mine), climb.at[1], climb_in.at[1], below)
    copies.start(row_piece(every, here, mine), hand.at[2], hand_in.at[2], mate)
    for d in NEAREST:
        copies.arrived(
            sides.at[k, lax.rem(z + NZ - d, NZ)], z2.at[d], z2_in.at[d], (row, lax.rem(z + d, NZ) * 2 + k)
        )
    copies.start(sides.at[k], mate2.at[0], mate2_in.at[0], mate)
    for n, part in enumerate((lower, upper)):
        ref = row_piece(part, share - here, mine)
        copies.arrived(ref, climb.at[n], climb_in.at[n], above)
        copies.start(ref, hand.at[n], hand_in.at[n], mate)
    copies.arrived(sides.at[1 - k], mate2.at[0], mate2_in.at[0], mate)
    for q in range(2):
        whole = jnp.concatenate([sides[core, chip, q] for chip in range(NZ) for core in range(2)], axis=0)
        value = jnp.dot(inv_factor[q], whole, preferred_element_type=jnp.float32)
        partial[q] = value.astype(jnp.bfloat16)
    for copy in late:
        copy.wait()
    copies.arrived(row_piece(every, here, theirs), hand.at[2], hand_in.at[2], mate)
    for n, part in enumerate((lower, upper)):
        copies.arrived(row_piece(part, share - here, theirs), hand.at[n], hand_in.at[n], mate)
    for plane in planes:
        plane.receive(2)
    copies.finish()


def gather(slots, number, panel_rows, panel, inv_factor, rhs, target, right_sides):
    dma = pltpu.SemaphoreType.DMA
    vmem = pl.BlockSpec(memory_space=pltpu.VMEM)
    hbm = pl.BlockSpec(memory_space=pltpu.MemorySpace.HBM)
    return pl.pallas_call(
        functools.partial(gather_kernel, slots),
        out_shape=(
            jax.ShapeDtypeStruct((NROW, slots, SLAB, PW), jnp.bfloat16),
            jax.ShapeDtypeStruct((NX, NY, slots, SLAB, PW), jnp.bfloat16),
            jax.ShapeDtypeStruct((2, PW, NRHS), jnp.bfloat16),
            jax.ShapeDtypeStruct((8, 256), jnp.int32),
            jax.ShapeDtypeStruct(target.shape, jnp.float32),
            jax.ShapeDtypeStruct(right_sides.shape, jnp.float32),
        ),
        in_specs=[hbm] * 6,
        out_specs=(vmem,) * 6,
        scratch_shapes=[
            pltpu.VMEM(panel_rows.shape, jnp.int32),
            pltpu.VMEM((2, 2, SLAB, PW), jnp.bfloat16),
            pltpu.VMEM((2, PW, PW), jnp.bfloat16),
            pltpu.VMEM((ZERO_BLOCK + 1, SLAB, PW), jnp.bfloat16),
            pltpu.VMEM((NROW, slots // 2, SLAB, PW // 2), jnp.bfloat16),
            pltpu.VMEM((2, NZ) + rhs.shape, jnp.bfloat16),
            pltpu.SMEM((8, 256), jnp.int32),
            dma((10,)), pltpu.SemaphoreType.REGULAR,
            dma((8,)), dma((8,)), dma((8,)), dma((8,)),
            dma((8,)), dma((8,)), dma((1,)), dma((1,)),
            dma((16,)), dma((16,)), dma((2,)), dma((2,)), dma((3,)), dma((3,)),
            dma((2, 4)), dma((2, 4)), dma((2, 4)), dma((2, 4)),
        ],
        compiler_params=pltpu.CompilerParams(
            collective_id=number, has_side_effects=True, vmem_limit_bytes=24 << 20
        ),
        name="gather_blocks",
    )(
        *[
            pltpu.with_memory_space_constraint(array, pltpu.MemorySpace.HBM)
            for array in (panel_rows, panel, inv_factor, rhs, target, right_sides)
        ]
    )


def update_kernel(
    slots,
    meta, rows, cols, partial, target, right_sides,
    out_target, out_sides,
    tiles, sides, left, right, product, tile_sem, side_sem,
):
    row = lax.axis_index("row") * 16
    col = lax.axis_index("col") * 16
    rows_here = meta[2, row]
    cols_here = meta[2, col]
    count = target.shape[0]

    def touched(base, total):
        bits = jnp.int32(0)
        for i in range(slots):
            bits |= jnp.where(i < total, jnp.int32(1) << (meta[1, base + i] & 7), 0)
        return bits

    row_bits = touched(row, rows_here)

    def send_tile(source, t):
        return pltpu.make_async_copy(source.at[t], out_target.at[t], tile_sem.at[t])

    for t in range(count):
        @pl.when(((row_bits >> t) & 1) == 0)
        def _():
            send_tile(target, t).start()

        @pl.when(((row_bits >> t) & 1) == 1)
        def _():
            tiles[t] = target[t]

    for i in range(slots):
        @pl.when(i < rows_here)
        def _():
            left[i * TILE:(i + 1) * TILE, :] = rows[:, i].reshape(TILE, PW)

        @pl.when(i < cols_here)
        def _():
            right[i * TILE:(i + 1) * TILE, :] = cols[:, i].reshape(TILE, PW)

    sides[...] = right_sides[...]

    half = slots // 2
    row_split, col_split = meta[4, row], meta[4, col]

    for q in range(2):
        row_from, row_to = (0, row_split) if q == 0 else (row_split, rows_here)
        col_from, col_to = (0, col_split) if q == 0 else (col_split, cols_here)

        def column_pair(jp, carry):
            j = col_from + jp * 2
            factor = right[pl.ds(pl.multiple_of(j * TILE, TILE), 2 * TILE), :]

            def row_group(part, carry):
                start = row_from + part * half
                product[...] = lax.dot_general(
                    left[pl.ds(pl.multiple_of(start * TILE, TILE), half * TILE), :],
                    factor,
                    (((1,), (1,)), ((), ())),
                    preferred_element_type=jnp.float32,
                )

                def subtract(i, carry):
                    t = meta[1, row + start + i] & 7
                    for b in range(2):
                        @pl.when(j + b < col_to)
                        def _():
                            at = (t, pl.ds(meta[1, col + j + b] & 7, TILE, 8), slice(None))
                            block = product[pl.ds(pl.multiple_of(i * TILE, TILE), TILE), b * TILE:(b + 1) * TILE]
                            tiles[at] = tiles[at] - block

                    return carry

                return lax.fori_loop(0, jnp.minimum(row_to - start, half), subtract, carry)

            return lax.fori_loop(0, (row_to - row_from + half - 1) // half, row_group, carry)

        lax.fori_loop(0, (col_to - col_from + 1) // 2, column_pair, 0)

    for t in range(count):
        @pl.when(((row_bits >> t) & 1) == 1)
        def _():
            send_tile(tiles, t).start()

    def side(j, carry):
        at = meta[1, col + j]
        product = jnp.dot(
            right[pl.ds(pl.multiple_of(j * TILE, TILE), TILE), :],
            partial[at >> 3],
            preferred_element_type=jnp.float32,
        )
        sides[at & 7] = sides[at & 7] - product
        return carry

    lax.fori_loop(0, cols_here, side, 0)
    last = pltpu.make_async_copy(sides, out_sides, side_sem)
    last.start()
    for t in range(count):
        send_tile(tiles, t).wait()
    last.wait()


def update(slots, meta, rows, cols, partial, target, right_sides):
    vmem = pl.BlockSpec(memory_space=pltpu.VMEM)
    hbm = pl.BlockSpec(memory_space=pltpu.MemorySpace.HBM)
    cols = cols.reshape(NROW, slots, SLAB, PW)
    return pl.pallas_call(
        functools.partial(update_kernel, slots),
        out_shape=(
            jax.ShapeDtypeStruct(target.shape, jnp.float32),
            jax.ShapeDtypeStruct(right_sides.shape, jnp.float32),
        ),
        in_specs=[pl.BlockSpec(memory_space=pltpu.SMEM)] + [vmem] * 5,
        out_specs=(hbm, hbm),
        scratch_shapes=[
            pltpu.VMEM(target.shape, jnp.float32),
            pltpu.VMEM(right_sides.shape, jnp.float32),
            pltpu.VMEM(((slots + slots // 2) * TILE, PW), jnp.bfloat16),
            pltpu.VMEM(((slots + 1) * TILE, PW), jnp.bfloat16),
            pltpu.VMEM((slots // 2 * TILE, 2 * TILE), jnp.float32),
            pltpu.SemaphoreType.DMA((8,)),
            pltpu.SemaphoreType.DMA,
        ],
        compiler_params=pltpu.CompilerParams(vmem_limit_bytes=30 << 20),
        name="update_blocks",
    )(meta, rows, cols, partial, target, right_sides)


def shards(target, panel_a, inv_factor, panel_rhs, panel_rows, right_sides):
    few, most = 10, 16
    args = (panel_rows, panel_a, inv_factor, panel_rhs, target.reshape(8, 1024, 128), right_sides.reshape(8, 128, 256))
    rows, cols, partial, meta, near_target, near_sides = gather(few, 0, *args)

    def usual():
        return update(few, meta, rows, cols, partial, near_target, near_sides)

    def crowded():
        rows, cols, partial, meta, near_target, near_sides = gather(most, 1, *args)
        return update(most, meta, rows, cols, partial, near_target, near_sides)

    new_target, new_sides = lax.cond(meta[3, 0] <= few, usual, crowded)
    return new_target.reshape(target.shape), new_sides.reshape(right_sides.shape)


def solution(mesh):
    placed = (
        P(None, "row", None, None, "col", None),
        P(None, "col", None, None),
        P(),
        P(None, "col", None),
        P(),
        P(None, "col", None, None),
    )
    return jax.shard_map(
        shards,
        mesh=mesh,
        in_specs=placed,
        out_specs=(P(None, "row", None, None, "col", None), P(None, "col", None, None)),
        check_vma=False,
    )
```

```python
import functools

import jax
import jax.numpy as jnp
from jax import lax
from jax.experimental import pallas as pl
from jax.experimental.pallas import tpu as pltpu
from jax.sharding import PartitionSpec as P

MESH = pl.DeviceIdType.MESH
NX, NY, NZ = 4, 4, 8
NROW, NCOL = 16, 16
SLAB = 8
PW = 512
NRHS = 256
TILE = 128
ZERO_BLOCK = 64
DISTANCES = (4, 3, 5, 2, 6, 1, 7)


def remote(src, dst, send_sem, recv_sem, device):
    return pltpu.make_async_remote_copy(
        src_ref=src, dst_ref=dst, send_sem=send_sem, recv_sem=recv_sem, device_id=device, device_id_type=MESH
    )


class Copies:
    def __init__(self):
        self.sent = []

    def start(self, ref, send_sem, recv_sem, device):
        copy = remote(ref, ref, send_sem, recv_sem, device)
        copy.start()
        self.sent.append(copy)

    def arrived(self, ref, send_sem, recv_sem, device):
        remote(ref, ref, send_sem, recv_sem, device).wait_recv()

    def finish(self, count=None):
        for copy in self.sent[:count]:
            copy.wait_send()
        self.sent = self.sent[count:] if count else []


class ZGather:
    def __init__(self, copies, piece, core, place, send, recv, mate_send, mate_recv):
        self.copies, self.piece, self.core = copies, piece, core
        self.row, self.z, self.k = place
        self.send, self.recv = send, recv
        self.mate_send, self.mate_recv = mate_send, mate_recv
        self.mate = (self.row, self.z * 2 + 1 - self.k)

    def chip(self, distance):
        return lax.rem(self.z + distance + NZ, NZ)

    def begin(self):
        own = self.piece(self.z * 2 + self.k)
        for d in DISTANCES:
            self.copies.start(own, self.send.at[d], self.recv.at[d], (self.row, self.chip(d) * 2 + self.k))

    def collect(self):
        for d in DISTANCES:
            ref = self.piece(self.chip(-d) * 2 + self.k)
            self.copies.arrived(ref, self.send.at[d], self.recv.at[d], (self.row, self.chip(d) * 2 + self.k))
        self.copies.start(self.core(self.k), self.mate_send.at[0], self.mate_recv.at[0], self.mate)

    def end(self):
        self.copies.arrived(self.core(1 - self.k), self.mate_send.at[0], self.mate_recv.at[0], self.mate)


class PlaneGather:
    def __init__(self, copies, cols, half, place, send1, recv1, send2, recv2):
        self.copies, self.cols, self.half = copies, cols, half
        self.x, self.y, self.col = place
        self.send1, self.recv1, self.send2, self.recv2 = send1, recv1, send2, recv2
        count = cols.shape[2] // 2
        self.slots = pl.ds(half * count, count)

    def move(self, stage, distance):
        along_x = (stage == 1) == (self.half == 0)
        x = lax.rem(self.x + distance + NX, NX) if along_x else self.x
        y = self.y if along_x else lax.rem(self.y + distance + NY, NY)
        return x, y

    def device(self, stage, distance):
        x, y = self.move(stage, distance)
        return (x * NY + y, self.col)

    def ref(self, stage, distance):
        x, y = self.move(stage, distance)
        if stage == 1:
            return self.cols.at[x, y, self.slots]
        return self.cols.at[:, y, self.slots] if self.half == 0 else self.cols.at[x, :, self.slots]

    def send(self, stage):
        sems = (self.send1, self.recv1) if stage == 1 else (self.send2, self.recv2)
        for d in (1, 3, 2):
            self.copies.start(self.ref(stage, 0), sems[0].at[d], sems[1].at[d], self.device(stage, d))

    def receive(self, stage):
        sems = (self.send1, self.recv1) if stage == 1 else (self.send2, self.recv2)
        for d in (1, 3, 2):
            self.copies.arrived(self.ref(stage, -d), sems[0].at[d], sems[1].at[d], self.device(stage, d))


def class_tables(panel_rows):
    count = panel_rows.shape[1]
    shape = (count, count)
    down = lax.broadcasted_iota(jnp.int32, shape, 0)
    across = lax.broadcasted_iota(jnp.int32, shape, 1)
    lane = lax.broadcasted_iota(jnp.int32, (count, 256), 1)
    block = lax.broadcasted_iota(jnp.int32, (count, 256), 0)
    wide = [jnp.broadcast_to(panel_rows[q:q + 1], shape) for q in range(2)]
    tall = [jnp.sum(jnp.where(down == across, w, 0), axis=1, keepdims=True) for w in wide]
    place, info, total = ZERO_BLOCK, 0, 0
    for q in range(2):
        same = (tall[q] & 15) == (wide[q] & 15)
        rank = jnp.sum(jnp.where(same & (across < down), 1, 0), axis=1, keepdims=True)
        if q == 1:
            rank += jnp.sum(jnp.where((tall[1] & 15) == (wide[0] & 15), 1, 0), axis=1, keepdims=True)
        hit = jnp.broadcast_to((tall[q] & 15) * 16 + rank, lane.shape) == lane
        where_from = ((block >> 1) & 1) * 32 + (block >> 2) * 4 + (block & 1) + q * 2
        place += jnp.sum(jnp.where(hit, where_from - ZERO_BLOCK, 0), axis=0, keepdims=True)
        spot = jnp.broadcast_to((tall[q] >> 4) + q * 8, lane.shape)
        info += jnp.sum(jnp.where(hit, spot, 0), axis=0, keepdims=True)
        member = jnp.broadcast_to(tall[q] & 15, lane.shape) == (lane >> 4)
        total += jnp.sum(jnp.where(member, 1, 0), axis=0, keepdims=True)
        if q == 0:
            lead = total
    most = jnp.broadcast_to(jnp.max(total, axis=1, keepdims=True), total.shape)
    return place, info, total, most, lead


def gather_kernel(
    slots,
    positions_hbm, panel, inv_hbm, rhs, target, right_sides,
    rows, cols, partial, meta, target_copy, sides_copy, largest,
    positions, slab, inv_factor, solved, picked, sides, table, local_sem, ready,
    z1, z1_in, mate1, mate1_in, z2, z2_in, mate2, mate2_in,
    swap, swap_in, climb, climb_in, hand, hand_in, plane1, plane1_in, plane2, plane2_in,
):
    row = lax.axis_index("row")
    col = lax.axis_index("col")
    x, y = row // NY, lax.rem(row, NY)
    z, k = col // 2, lax.rem(col, 2)
    place = (row, z, k)
    mate = (row, z * 2 + 1 - k)

    def load(src, dst, n):
        copy = pltpu.make_async_copy(src, dst, local_sem.at[n])
        copy.start()
        return copy

    own_rows = pl.ds(pl.multiple_of(row * SLAB, SLAB), SLAB)
    first = [load(panel.at[q, b, own_rows], slab.at[q, b], 2 * q + b) for q in range(2) for b in range(2)]
    first += [load(inv_hbm, inv_factor, 4)]
    second = [load(rhs, sides.at[k, z], 5), load(positions_hbm, positions, 9)]

    barrier = pltpu.get_barrier_semaphore()
    partners = [(row, lax.rem(z + d, NZ) * 2 + k) for d in DISTANCES] + [mate]
    ring_x = [(lax.rem(x + d, NX) * NY + y, col) for d in range(1, NX)]
    ring_y = [(x * NY + lax.rem(y + d, NY), col) for d in range(1, NY)]
    partners += ring_x + ring_y
    for partner in partners:
        pl.semaphore_signal(barrier, inc=1, device_id=partner, device_id_type=MESH)

    solved[ZERO_BLOCK] = jnp.zeros((SLAB, PW), jnp.bfloat16)
    for copy in first:
        copy.wait()
    for q in range(2):
        block = slab[q].astype(jnp.float32).reshape(2 * SLAB, PW).astype(jnp.bfloat16)
        value = lax.dot_general(
            block, inv_factor[q], (((1,), (1,)), ((), ())), preferred_element_type=jnp.float32
        )
        for b in range(2):
            solved[k * 32 + z * 4 + q * 2 + b] = value[b * SLAB:(b + 1) * SLAB].astype(jnp.bfloat16)
    for copy in second:
        copy.wait()

    late = [load(target, target_copy, 6), load(right_sides, sides_copy, 7)]
    pl.semaphore_wait(barrier, len(partners))

    copies = Copies()
    slabs = ZGather(
        copies, lambda origin: solved.at[pl.ds(lax.rem(origin, 2) * 32 + (origin // 2) * 4, 4)],
        lambda core: solved.at[pl.ds(core * 32, 32)], place, z1, z1_in, mate1, mate1_in
    )
    planes = [
        PlaneGather(
            copies, cols, half, (x, y, col), plane1.at[half], plane1_in.at[half], plane2.at[half], plane2_in.at[half]
        )
        for half in range(2)
    ]

    slabs.begin()
    for partner in ring_x:
        pl.semaphore_signal(ready, inc=1, device_id=partner, device_id_type=MESH)
    for n, values in enumerate(class_tables(positions[...])):
        meta[n:n + 1, :] = values
    to_scalars = load(meta, table, 8)
    to_scalars.wait()
    largest[0] = table[3, 0]
    slabs.collect()
    slabs.end()
    pl.semaphore_wait(ready, len(ring_x))

    share = slots // 2
    width = PW // 2
    mine = pl.ds(pl.multiple_of(k * width, width), width)
    theirs = pl.ds(pl.multiple_of((1 - k) * width, width), width)
    here = lax.rem(z, 2) * share
    above = (row, lax.rem(z + 1, NZ) * 2 + k)
    below = (row, lax.rem(z + NZ - 1, NZ) * 2 + k)

    def row_piece(slabs_from, start, columns):
        return rows.at[slabs_from, pl.ds(start, share), :, columns]

    def send_rows(d, carry):
        there = lax.rem(row + d, NROW)
        for j in range(share):
            picked[d, j] = solved[table[0, there * 16 + here + j], :, mine]
        remote(picked.at[d], row_piece(row, here, mine), swap.at[d], swap_in.at[d], (there, col)).start()
        return carry

    every = pl.ds(0, NROW)
    lower, upper = pl.ds(0, NROW // 2), pl.ds(NROW // 2, NROW // 2)

    def receive_rows(d, carry):
        ref = row_piece(lax.rem(row + NROW - d, NROW), here, mine)
        remote(picked.at[d], ref, swap.at[d], swap_in.at[d], (lax.rem(row + d, NROW), col)).wait()
        return carry

    for slot in range(slots):
        cols[x, y, slot] = solved[table[0, col * 16 + slot]]
    for plane in planes:
        plane.send(1)
    lax.fori_loop(1, NROW, send_rows, 0)
    for j in range(share):
        rows[row, here + j, :, mine] = solved[table[0, row * 16 + here + j], :, mine]
    for d in DISTANCES:
        copies.start(sides.at[k, z], z2.at[d], z2_in.at[d], (row, lax.rem(z + d, NZ) * 2 + k))
    early = len(copies.sent)
    for plane in planes:
        plane.receive(1)
        plane.send(2)
    lax.fori_loop(1, NROW, receive_rows, 0)
    copies.start(row_piece(lower, here, mine), climb.at[0], climb_in.at[0], above)
    copies.start(row_piece(upper, here, mine), climb.at[1], climb_in.at[1], below)
    copies.start(row_piece(every, here, mine), hand.at[2], hand_in.at[2], mate)
    copies.finish(early)
    for d in DISTANCES:
        copies.arrived(
            sides.at[k, lax.rem(z + NZ - d, NZ)], z2.at[d], z2_in.at[d], (row, lax.rem(z + d, NZ) * 2 + k)
        )
    copies.start(sides.at[k], mate2.at[0], mate2_in.at[0], mate)
    for n, part in enumerate((lower, upper)):
        ref = row_piece(part, share - here, mine)
        copies.arrived(ref, climb.at[n], climb_in.at[n], above)
        copies.start(ref, hand.at[n], hand_in.at[n], mate)
    copies.arrived(sides.at[1 - k], mate2.at[0], mate2_in.at[0], mate)
    for q in range(2):
        whole = jnp.concatenate([sides[core, chip, q] for chip in range(NZ) for core in range(2)], axis=0)
        value = jnp.dot(inv_factor[q], whole, preferred_element_type=jnp.float32)
        partial[q] = value.astype(jnp.bfloat16)
    for copy in late:
        copy.wait()
    copies.arrived(row_piece(every, here, theirs), hand.at[2], hand_in.at[2], mate)
    for n, part in enumerate((lower, upper)):
        copies.arrived(row_piece(part, share - here, theirs), hand.at[n], hand_in.at[n], mate)
    for plane in planes:
        plane.receive(2)
    copies.finish()


def gather(slots, number, panel_rows, panel, inv_factor, rhs, target, right_sides):
    dma = pltpu.SemaphoreType.DMA
    vmem = pl.BlockSpec(memory_space=pltpu.VMEM)
    hbm = pl.BlockSpec(memory_space=pltpu.MemorySpace.HBM)
    return pl.pallas_call(
        functools.partial(gather_kernel, slots),
        out_shape=(
            jax.ShapeDtypeStruct((NROW, slots, SLAB, PW), jnp.bfloat16),
            jax.ShapeDtypeStruct((NX, NY, slots, SLAB, PW), jnp.bfloat16),
            jax.ShapeDtypeStruct((2, PW, NRHS), jnp.bfloat16),
            jax.ShapeDtypeStruct((8, 256), jnp.int32),
            jax.ShapeDtypeStruct(target.shape, jnp.float32),
            jax.ShapeDtypeStruct(right_sides.shape, jnp.float32),
            jax.ShapeDtypeStruct((1,), jnp.int32),
        ),
        in_specs=[hbm] * 6,
        out_specs=(vmem,) * 6 + (pl.BlockSpec(memory_space=pltpu.SMEM),),
        scratch_shapes=[
            pltpu.VMEM(panel_rows.shape, jnp.int32),
            pltpu.VMEM((2, 2, SLAB, PW), jnp.bfloat16),
            pltpu.VMEM((2, PW, PW), jnp.bfloat16),
            pltpu.VMEM((ZERO_BLOCK + 1, SLAB, PW), jnp.bfloat16),
            pltpu.VMEM((NROW, slots // 2, SLAB, PW // 2), jnp.bfloat16),
            pltpu.VMEM((2, NZ) + rhs.shape, jnp.bfloat16),
            pltpu.SMEM((8, 256), jnp.int32),
            dma((10,)), pltpu.SemaphoreType.REGULAR,
            dma((8,)), dma((8,)), dma((8,)), dma((8,)),
            dma((8,)), dma((8,)), dma((1,)), dma((1,)),
            dma((16,)), dma((16,)), dma((2,)), dma((2,)), dma((3,)), dma((3,)),
            dma((2, 4)), dma((2, 4)), dma((2, 4)), dma((2, 4)),
        ],
        compiler_params=pltpu.CompilerParams(
            collective_id=number, has_side_effects=True, vmem_limit_bytes=24 << 20
        ),
        name="gather_blocks",
    )(
        *[
            pltpu.with_memory_space_constraint(array, pltpu.MemorySpace.HBM)
            for array in (panel_rows, panel, inv_factor, rhs, target, right_sides)
        ]
    )


def update_kernel(
    slots,
    meta, rows, cols, partial, target, right_sides,
    out_target, out_sides,
    tiles, sides, left, right, product, tile_sem, side_sem,
):
    row = lax.axis_index("row") * 16
    col = lax.axis_index("col") * 16
    rows_here = meta[2, row]
    cols_here = meta[2, col]
    count = target.shape[0]

    def touched(base, total):
        bits = jnp.int32(0)
        for i in range(slots):
            bits |= jnp.where(i < total, jnp.int32(1) << (meta[1, base + i] & 7), 0)
        return bits

    row_bits = touched(row, rows_here)

    def send_tile(source, t):
        return pltpu.make_async_copy(source.at[t], out_target.at[t], tile_sem.at[t])

    for t in range(count):
        @pl.when(((row_bits >> t) & 1) == 0)
        def _():
            send_tile(target, t).start()

        @pl.when(((row_bits >> t) & 1) == 1)
        def _():
            tiles[t] = target[t]

    for i in range(slots):
        @pl.when(i < rows_here)
        def _():
            left[i * TILE:(i + 1) * TILE, :] = rows[:, i].reshape(TILE, PW)

        @pl.when(i < cols_here)
        def _():
            right[i * TILE:(i + 1) * TILE, :] = cols[:, i].reshape(TILE, PW)

    sides[...] = right_sides[...]

    half = slots // 2
    row_split, col_split = meta[4, row], meta[4, col]

    for q in range(2):
        row_from, row_to = (0, row_split) if q == 0 else (row_split, rows_here)
        col_from, col_to = (0, col_split) if q == 0 else (col_split, cols_here)

        def column_pair(jp, carry):
            j = col_from + jp * 2
            factor = right[pl.ds(pl.multiple_of(j * TILE, TILE), 2 * TILE), :]

            def row_group(part, carry):
                start = row_from + part * half
                product[...] = lax.dot_general(
                    left[pl.ds(pl.multiple_of(start * TILE, TILE), half * TILE), :],
                    factor,
                    (((1,), (1,)), ((), ())),
                    preferred_element_type=jnp.float32,
                )

                def subtract(i, carry):
                    t = meta[1, row + start + i] & 7
                    for b in range(2):
                        @pl.when(j + b < col_to)
                        def _():
                            at = (t, pl.ds(meta[1, col + j + b] & 7, TILE, 8), slice(None))
                            block = product[pl.ds(pl.multiple_of(i * TILE, TILE), TILE), b * TILE:(b + 1) * TILE]
                            tiles[at] = tiles[at] - block

                    return carry

                return lax.fori_loop(0, jnp.minimum(row_to - start, half), subtract, carry)

            return lax.fori_loop(0, (row_to - row_from + half - 1) // half, row_group, carry)

        lax.fori_loop(0, (col_to - col_from + 1) // 2, column_pair, 0)

    for t in range(count):
        @pl.when(((row_bits >> t) & 1) == 1)
        def _():
            send_tile(tiles, t).start()

    def side(j, carry):
        at = meta[1, col + j]
        product = jnp.dot(
            right[pl.ds(pl.multiple_of(j * TILE, TILE), TILE), :],
            partial[at >> 3],
            preferred_element_type=jnp.float32,
        )
        sides[at & 7] = sides[at & 7] - product
        return carry

    lax.fori_loop(0, cols_here, side, 0)
    last = pltpu.make_async_copy(sides, out_sides, side_sem)
    last.start()
    for t in range(count):
        send_tile(tiles, t).wait()
    last.wait()


def update(slots, meta, rows, cols, partial, target, right_sides):
    vmem = pl.BlockSpec(memory_space=pltpu.VMEM)
    hbm = pl.BlockSpec(memory_space=pltpu.MemorySpace.HBM)
    cols = cols.reshape(NROW, slots, SLAB, PW)
    return pl.pallas_call(
        functools.partial(update_kernel, slots),
        out_shape=(
            jax.ShapeDtypeStruct(target.shape, jnp.float32),
            jax.ShapeDtypeStruct(right_sides.shape, jnp.float32),
        ),
        in_specs=[pl.BlockSpec(memory_space=pltpu.SMEM)] + [vmem] * 5,
        out_specs=(hbm, hbm),
        scratch_shapes=[
            pltpu.VMEM(target.shape, jnp.float32),
            pltpu.VMEM(right_sides.shape, jnp.float32),
            pltpu.VMEM(((slots + slots // 2) * TILE, PW), jnp.bfloat16),
            pltpu.VMEM(((slots + 1) * TILE, PW), jnp.bfloat16),
            pltpu.VMEM((slots // 2 * TILE, 2 * TILE), jnp.float32),
            pltpu.SemaphoreType.DMA((8,)),
            pltpu.SemaphoreType.DMA,
        ],
        compiler_params=pltpu.CompilerParams(vmem_limit_bytes=30 << 20),
        name="update_blocks",
    )(meta, rows, cols, partial, target, right_sides)


def shards(target, panel_a, inv_factor, panel_rhs, panel_rows, right_sides):
    few, most = 10, 16
    args = (panel_rows, panel_a, inv_factor, panel_rhs, target.reshape(8, 1024, 128), right_sides.reshape(8, 128, 256))
    rows, cols, partial, meta, near_target, near_sides, largest = gather(few, 0, *args)

    def usual():
        return update(few, meta, rows, cols, partial, near_target, near_sides)

    def crowded():
        rows, cols, partial, meta, near_target, near_sides, _ = gather(most, 1, *args)
        return update(most, meta, rows, cols, partial, near_target, near_sides)

    new_target, new_sides = lax.cond(largest[0] <= few, usual, crowded)
    return new_target.reshape(target.shape), new_sides.reshape(right_sides.shape)


def solution(mesh):
    placed = (
        P(None, "row", None, None, "col", None),
        P(None, "col", None, None),
        P(),
        P(None, "col", None),
        P(),
        P(None, "col", None, None),
    )
    return jax.shard_map(
        shards,
        mesh=mesh,
        in_specs=placed,
        out_specs=(P(None, "row", None, None, "col", None), P(None, "col", None, None)),
        check_vma=False,
    )
```
